32 devices in a mesh: group: 2 (over y), ctx: 4 (over z), dp: 4 (over x, core).
Axes of the slice: x: 2, y: 2, z: 4, core: 2. Of those that a mesh axis runs over, the one named last changes fastest.
Arguments:
- queries: bfloat16 [8, 512, 2048], P(('group', 'dp'), 'ctx'), parts along dimension 0, may hold values from -6 to 6
- keys: bfloat16 [8, 512, 2048], P(('group', 'dp'), 'ctx'), parts along dimension 0, may hold values from -6 to 6
- values: bfloat16 [8, 512, 2048], P(('group', 'dp'), 'ctx'), parts along dimension 0, may hold values from -6 to 6
- grad_normed: bfloat16 [8, 512, 2048], P(('group', 'dp'), 'ctx'), parts along dimension 0, may hold values from -6 to 6
- gain: bfloat16 [2048], replicated, may hold values from 0.5 to 1.5
- doc_ids: int32 [8, 4], P(('group', 'dp'), 'ctx'), parts along dimension 0, may hold values from 0 to 2, never falling along the last dimension, each value on 1 to 2 neighbouring positions
Outputs:
- grad_queries: bfloat16 [8, 512, 2048], P(('group', 'dp'), 'ctx'), parts along dimension 0
- grad_keys: bfloat16 [8, 512, 2048], P(('group', 'dp'), 'ctx'), parts along dimension 0
- grad_values: bfloat16 [8, 512, 2048], P(('group', 'dp'), 'ctx'), parts along dimension 0
- grad_gain: float32 [4096], P(('group', 'dp')), parts along dimension 0
The draws below stay inside these ranges and needn't reach their ends.
There are 2 independent parts, one for each index of `group`. The reference program is written for one: setup_inputs(seed, part) draws one part's arguments, and reference() takes and returns one part's arrays. A program takes and returns all parts, laid end to end along the dimension named above; an argument that names none is the same for every part. Nothing has to cross between parts.
Inputs may be any that keep to these rules, and one draw needn't show every extreme that they name: `doc_ids`: along each sequence the document numbers never fall; every number from 0 to 2 appears, and one document holds exactly 2 spans.
All inputs are finite; a program needn't handle non-finite values.
Results may differ from the reference program's by a relative error of at most 0.0058.
Values sent between devices are 32-bit elements; how exact they have to be, the bound alone decides.
A program may use at most 64 MiB of HBM per device.

```python
import math
import jax
import jax.numpy as jnp
import numpy as np
from jax import lax

HEADS = 16
HEAD_DIM = 128
SPAN = 128
HD = 2048
LENGTH = 512
SEQS = 4
SPANS = 4


def strengthened(values, rng, source, target, blocks, factor):
    def block_of(dim):
        return (jnp.arange(values.shape[dim]) // (values.shape[dim] // blocks)).reshape((-1,) + (1,) * (values.ndim - 1 - dim))

    first = jax.random.permutation(rng, blocks)[block_of(target)]
    other_side = (block_of(target) + blocks // 2) % blocks
    return jnp.where((block_of(source) == first) | (block_of(source) == other_side), factor * values, values)


def block_levels(own_key, dims, pieces, low, high):
    def one(position, blocks):
        draws = jax.random.uniform(jax.random.fold_in(jax.random.fold_in(own_key, 6), position), (blocks,), jnp.float32, low / len(pieces), high / len(pieces))
        return jnp.repeat(jnp.exp(draws), dims[position] // blocks).reshape((-1,) + (1,) * (len(dims) - position - 1))

    factor_of = one(*pieces[0])
    for cut in pieces[1:]:
        factor_of = factor_of * one(*cut)
    return factor_of


def profile(number_of, total, most, slope):
    portions = [(1 << 20) // math.isqrt(grade ** slope) + 1 for grade in range(2, number_of + 1)]
    rest, holding = total - most - (number_of - 1), [1] * (number_of - 1)
    while rest > 0:
        candidates = [i for i in range(number_of - 1) if holding[i] < most]
        whole, budget = sum([portions[i] for i in candidates]), rest
        for i in candidates:
            addition = min(most - holding[i], max(1, budget * portions[i] // whole), rest)
            holding[i] = holding[i] + addition
            rest = rest - addition
    return np.array([most] + holding)


def uneven(key, amount, total, reach, slope):
    if amount == 2:
        one = jax.random.randint(key, (), max(1, total - reach), min(reach, total - 1) + 1)
        return jnp.stack([one, total - one])
    tallies = jnp.asarray(profile(amount, total, reach, slope), jnp.int32)
    twos = (amount - 1) // 2
    source_of, receiver = tallies[1:1 + 2 * twos:2], tallies[2:2 + 2 * twos:2]
    room = jnp.minimum(source_of - 1, reach - receiver)
    moved = jax.random.randint(jax.random.fold_in(key, 1), (twos,), 0, 1 << 20) % (room + 1)
    tallies = tallies.at[1:1 + 2 * twos:2].set(source_of - moved).at[2:2 + 2 * twos:2].set(receiver + moved)
    return tallies[jax.random.permutation(jax.random.fold_in(key, 2), amount)]


def noise(stream_key, dims, deviation, bound, shards=(), dtype=jnp.bfloat16):
    drawn = jax.random.normal(stream_key, dims, jnp.float32) * deviation
    if len(shards) > 0:
        drawn = block_levels(stream_key, dims, shards, -0.22, 0.18) * drawn
    return jnp.clip(drawn, min=-bound, max=bound).astype(dtype)


def heavy_noise(own_key, dims, spread, bound, pieces, heavy, held_as=jnp.bfloat16):
    array = spread * jax.random.normal(own_key, dims, jnp.float32)
    if pieces:
        array = array * block_levels(own_key, dims, pieces, -0.22, 0.18)
    return jnp.clip(strengthened(array, jax.random.fold_in(own_key, 3), *heavy), -bound, bound).astype(held_as)


def setup_inputs(seed: int = 0, part: int = 0) -> dict:
    key_of = jax.random.split(jax.random.key(seed), 7)
    own_keys = jax.random.split(jax.random.fold_in(key_of[6], part), 7)
    queries = noise(own_keys[0], (SEQS, LENGTH, HD), 1.0, 6.0, ((0, 4), (1, 4)))
    keys = noise(own_keys[1], (SEQS, LENGTH, HD), 1.0, 6.0, ((0, 4), (1, 4)))
    values = noise(own_keys[2], (SEQS, LENGTH, HD), 1.0, 6.0, ((0, 4), (1, 4)))
    grad_normed = heavy_noise(own_keys[3], (SEQS, LENGTH, HD), 1.0, 6.0, ((0, 4), (1, 4)), (0, 2, 4, 2.0))
    gain = jnp.clip(1.0 + 0.1 * jax.random.normal(key_of[4], (HD,), jnp.float32), 0.5, 1.5).astype(jnp.bfloat16)
    doc_ids = jax.vmap(lambda own: jnp.searchsorted(jnp.cumsum(uneven(own, 3, SPANS, SPANS // 2, 2)), jnp.arange(SPANS), side="right"))(jax.random.split(own_keys[5], SEQS)).reshape((SEQS, SPANS)).astype(jnp.int32)
    return {"queries": queries, "keys": keys, "values": values, "grad_normed": grad_normed, "gain": gain, "doc_ids": doc_ids}


def linked_sum(terms, tags, reverse):

    def advance(carry, item):
        state, last = carry
        term, tag = item
        enter = jnp.where(tag == last, state, jnp.zeros_like(state))
        return ((enter + term, tag), enter)
    start = (jnp.zeros(terms.shape[1:], jnp.float32), jnp.float32(0.0))
    _, entering = lax.scan(advance, start, (terms, tags), reverse=reverse)
    return entering

def round_keep(value):
    return lax.optimization_barrier(value.astype(jnp.bfloat16)).astype(jnp.float32)

def mix(form, left, right):
    return jnp.einsum(form, left, right, precision=lax.Precision.HIGHEST)

def reference(queries, keys, values, grad_normed, gain, doc_ids):
    gain32 = gain.astype(jnp.float32)
    causal = jnp.tril(jnp.ones((SPAN, SPAN), jnp.bool_))

    def one_sequence(items):
        qrow, krow, vrow, grow, drow = items
        count = qrow.shape[0] // SPAN
        shape = (count, SPAN, HEADS, HEAD_DIM)
        qf = qrow.astype(jnp.float32).reshape(shape)
        kf = krow.astype(jnp.float32).reshape(shape)
        vf = vrow.astype(jnp.float32).reshape(shape)
        tags = (drow + 1).astype(jnp.float32)
        scores = mix('cthd,cshd->chts', qf, kf)
        intra = round_keep(jnp.where(causal, scores, 0.0))
        kv_terms = mix('cthd,cthe->chde', kf, vf)
        state_b = round_keep(linked_sum(kv_terms, tags, False))
        attn = mix('chts,cshe->cthe', intra, vf) + mix('cthd,chde->cthe', qf, state_b)
        attn = attn.reshape(qrow.shape)
        inv = 1.0 / jnp.sqrt(lax.optimization_barrier(jnp.mean(attn * attn, axis=-1, keepdims=True)) + 1e-05)
        gradf = grow.astype(jnp.float32)
        gain_term = lax.optimization_barrier(jnp.sum(gradf * attn * inv, axis=0))
        upper = gradf * gain32
        inner = lax.optimization_barrier(jnp.sum(upper * attn, axis=-1, keepdims=True))
        grad_attn = round_keep(upper * inv - attn * inner * inv ** 3 / HD).reshape(shape)
        grad_intra = round_keep(jnp.where(causal, mix('cthe,cshe->chts', grad_attn, vf), 0.0))
        qdo_terms = mix('cthd,cthe->chde', qf, grad_attn)
        back_b = round_keep(linked_sum(qdo_terms, tags, True))
        grad_q = mix('chts,cshd->cthd', grad_intra, kf) + mix('cthe,chde->cthd', grad_attn, state_b)
        grad_k = mix('chts,cthd->cshd', grad_intra, qf) + mix('cshe,chde->cshd', vf, back_b)
        grad_v = mix('chts,cthe->cshe', intra, grad_attn) + mix('cshd,chde->cshe', kf, back_b)
        flat = qrow.shape
        return (grad_q.reshape(flat).astype(jnp.bfloat16), grad_k.reshape(flat).astype(jnp.bfloat16), grad_v.reshape(flat).astype(jnp.bfloat16), gain_term)
    grad_q, grad_k, grad_v, gain_terms = lax.map(one_sequence, (queries, keys, values, grad_normed, doc_ids))
    return (grad_q, grad_k, grad_v, lax.optimization_barrier(jnp.sum(gain_terms, axis=0)))
```

```python
import functools

import jax
import jax.numpy as jnp
from jax import lax
from jax.experimental import pallas as pl
from jax.experimental.pallas import tpu as pltpu
from jax.sharding import PartitionSpec as P

HEADS = 16
DIM = 128
SPAN = 128
SHIFT = 3
GROUP = 4
MESH = pl.DeviceIdType.MESH
F32 = jnp.float32
BF16 = jnp.bfloat16


def dot(a, b, ca, cb):
    return lax.dot_general(a, b, (((ca,), (cb,)), ((), ())), preferred_element_type=F32)


def kernel(
    n, ndp, chain, shift, doc, gain_hbm, q_hbm, k_hbm, v_hbm, y_hbm,
    gq, gk, gv, gg_out,
    gain_in, gain, q, k, v, y, kvb, kvr, intra, attn, da, stb, qdo, bkr, gkp, gvp,
    tag, tagl, tagr, ssq, inn, gsum, ga, gb, stage, rstage, dsq, dnn, stat, statr, scal, scalr,
    in_sem, ks, kr, bs, br, ts, tr, gas, gar, gbs, gbr, ss, sr, ms, mr, gate, ready,
):
    me = lax.axis_index("ctx")
    mydp = lax.axis_index("dp")
    right, left = lax.rem(me + 1, n), lax.rem(me + n - 1, n)
    has_right, has_left = me < n - 1, me > 0
    lead = lax.rem(mydp, 2) == 0
    follow = jnp.logical_not(lead)
    twin = mydp + 1 - 2 * lax.rem(mydp, 2)
    hps = HEADS // ndp
    plain = HEADS - shift
    features = HEADS * DIM

    loads = [
        pltpu.make_async_copy(src, dst, in_sem.at[i])
        for i, (src, dst) in enumerate(
            ((k_hbm, k), (v_hbm, v), (q_hbm, q), (y_hbm, y), (gain_hbm, gain_in))
        )
    ]
    for load in loads:
        load.start()

    barrier = pltpu.get_barrier_semaphore()

    def greet(sem, axis, place, inside):
        @pl.when(inside)
        def _():
            pl.semaphore_signal(sem, inc=1, device_id={axis: place}, device_id_type=MESH)

    for o in range(1, n):
        greet(barrier, "ctx", lax.rem(me + o, n), me + o < n)
    greet(barrier, "ctx", left, has_left)
    for o in range(1, ndp):
        greet(barrier, "dp", lax.rem(mydp + o, ndp), mydp + o < ndp)

    def cols(h):
        return pl.ds(pl.multiple_of(h * DIM, DIM), DIM)

    def loop(first, last, body, group=GROUP):
        whole = (last - first) // group

        def step(g, _):
            body([first + g * group + i for i in range(group)])
            return 0

        if whole == 1:
            step(0, 0)
        elif whole > 1:
            lax.fori_loop(0, whole, step, 0)
        if first + whole * group < last:
            body(list(range(first + whole * group, last)))

    def each(first, last, body):
        def step(h, _):
            body(h)
            return 0

        if last > first:
            lax.fori_loop(first, last, step, 0)

    def remote(src, dst, s, r, where):
        return pltpu.make_async_remote_copy(
            src_ref=src, dst_ref=dst, send_sem=s, recv_sem=r, device_id=where, device_id_type=MESH
        )

    to_right, to_left = {"ctx": right}, {"ctx": left}

    def kv_copy(h):
        return remote(kvb.at[h], kvr.at[h], ks.at[h], kr.at[h], to_right)

    def back_copy(h):
        return remote(qdo.at[h], bkr.at[h], bs.at[h], br.at[h], to_left)

    def pair_copy(j):
        return remote(stage.at[j, 0:2], rstage.at[j, 0:2], ss.at[j, 0], sr.at[j, 0], to_left)

    def local_copy(j):
        return remote(stage.at[j, 2], rstage.at[j, 2], ss.at[j, 1], sr.at[j, 1], to_left)

    def opened(i):
        pl.semaphore_signal(gate.at[i], inc=1, device_id={"dp": twin}, device_id_type=MESH)

    tag_right = remote(tag, tagl, ts.at[0], tr.at[0], to_right)
    tag_left = remote(tag, tagr, ts.at[1], tr.at[1], to_left)
    stat_right = remote(stat, statr, ms.at[0], mr.at[0], to_right)
    scal_left = remote(scal, scalr, ms.at[1], mr.at[1], to_left)

    own = (doc[0, 0] + 1).astype(F32)
    tag[...] = jnp.full((8, 128), own, F32)
    ssq[...] = jnp.zeros_like(ssq)
    inn[...] = jnp.zeros_like(inn)
    dsq[...] = jnp.zeros_like(dsq)
    dnn[...] = jnp.zeros_like(dnn)

    @pl.when(jnp.logical_not(has_left))
    def _():
        tagl[...] = jnp.full((8, 128), -1.0, F32)
        kvr[...] = jnp.zeros_like(kvr)
        statr[...] = jnp.zeros_like(statr)

    @pl.when(jnp.logical_not(has_right))
    def _():
        tagr[...] = jnp.full((8, 128), -1.0, F32)
        bkr[...] = jnp.zeros_like(bkr)

    rows = lax.broadcasted_iota(jnp.int32, (SPAN, SPAN), 0)
    lanes = lax.broadcasted_iota(jnp.int32, (SPAN, SPAN), 1)
    causal = rows >= lanes

    loads[0].wait()
    loads[1].wait()
    pl.semaphore_wait(barrier, me + jnp.where(has_right, 1, 0) + mydp)
    for o in range(2, n):
        greet(ready, "ctx", lax.rem(me + n - o, n), me >= o)
    for o in range(1, ndp):
        greet(ready, "dp", lax.rem(mydp + ndp - o, ndp), mydp >= o)

    @pl.when(has_right)
    def _():
        tag_right.start()

    @pl.when(has_left)
    def _():
        tag_left.start()

    def kv_only(hs):
        for h, m in [(h, dot(k[:, cols(h)], v[:, cols(h)], 0, 0)) for h in hs]:
            kvb[h] = m

    def kv_step(hs):
        kv_only(hs)
        if not chain:

            @pl.when(jnp.logical_and(has_right, lead))
            def _():
                for h in hs:
                    kv_copy(h).start()

    def local_step(hs):
        scores = [dot(q[:, cols(h)], k[:, cols(h)], 1, 1) for h in hs]
        ws = [jnp.where(causal, x, 0.0).astype(BF16) for x in scores]
        outs = [dot(w, v[:, cols(h)], 1, 0) for h, w in zip(hs, ws)]
        for h, w, a in zip(hs, ws, outs):
            intra[:, cols(h)] = w
            attn[:, cols(h)] = a
        return outs

    def sums(terms):
        total = terms[0]
        for term in terms[1:]:
            total = total + term
        return total

    def norm_sums(hs, outs):
        ssq[...] += sums([a * a for a in outs])
        inn[...] += sums([y[:, cols(h)].astype(F32) * gain[h] * a for h, a in zip(hs, outs)])

    def stage_step(js):
        hs = [plain + j for j in js]
        for j, h in zip(js, hs):
            stage[j, 0] = q[:, cols(h)].astype(F32)
            stage[j, 1] = y[:, cols(h)].astype(F32)

        @pl.when(jnp.logical_and(has_left, lead))
        def _():
            for j in js:
                pair_copy(j).start()

        outs = local_step(hs)
        for j, a in zip(js, outs):
            stage[j, 2] = a

        @pl.when(jnp.logical_and(has_left, lead))
        def _():
            for j in js:
                local_copy(j).start()

        norm_sums(hs, outs)

    ahead = min(GROUP, plain)
    loop(0, ahead, kv_step)
    for load in loads[2:]:
        load.wait()
    for h in range(HEADS):
        gain[h] = gain_in[h * DIM : (h + 1) * DIM].astype(F32).reshape(1, DIM)
    loop(0, shift, stage_step, 1)
    loop(ahead, plain, kv_step)
    loop(plain, HEADS, kv_only)
    loop(0, plain, local_step)

    later = jnp.where(has_right, n - 2 - me, 0) + ndp - 1 - mydp

    @pl.when(later > 0)
    def _():
        pl.semaphore_wait(ready, later)

    if not chain:

        @pl.when(follow)
        def _():
            pl.semaphore_wait(gate.at[0], 1)

            @pl.when(has_left)
            def _():
                for j in range(shift):
                    pair_copy(j).start()
                    local_copy(j).start()

            pl.semaphore_wait(gate.at[1], 1)

            @pl.when(has_right)
            def _():
                each(0, plain, lambda h: kv_copy(h).start())

    @pl.when(has_left)
    def _():
        tag_right.wait_recv()

    @pl.when(has_right)
    def _():
        tag_left.wait_recv()

    from_left = jnp.broadcast_to(tagl[0:1, :] == tag[0:1, :], (DIM, DIM))
    from_right = jnp.broadcast_to(tagr[0:1, :] == tag[0:1, :], (DIM, DIM))

    def state_step(hs):
        @pl.when(has_left)
        def _():
            for h in hs:
                kv_copy(h).wait_recv()

        states = [jnp.where(from_left, kvr[h], 0.0) for h in hs]
        if chain:
            for h, state in zip(hs, states):
                kvb[h] = kvb[h] + state

            @pl.when(has_right)
            def _():
                for h in hs:
                    kv_copy(h).start()

        rounded = [state.astype(BF16) for state in states]
        outs = [attn[:, cols(h)] + dot(q[:, cols(h)], sb, 1, 0) for h, sb in zip(hs, rounded)]
        for h, sb, a in zip(hs, rounded, outs):
            stb[h] = sb
            attn[:, cols(h)] = a
        return outs

    def attn_step(hs):
        norm_sums(hs, state_step(hs))

    def helper_step(js):
        for j in js:
            pair_copy(j).wait_recv()
            local_copy(j).wait_recv()
        kbs = [jnp.where(from_right, kvb[plain + j], 0.0).astype(BF16) for j in js]
        xs = [dot(rstage[j, 0].astype(BF16), kb, 1, 0) for j, kb in zip(js, kbs)]
        olds = [rstage[j, 2] for j in js]
        dsq[...] += sums([(2.0 * a + x) * x for a, x in zip(olds, xs)])
        dnn[...] += sums([rstage[j, 1] * gain[plain + j] * x for j, x in zip(js, xs)])
        for j, a, x in zip(js, olds, xs):
            rstage[j, 2] = a + x

    early, gated = shift - 2, plain - 3
    if shift:
        for p in range(shift):
            loop(gated * p // shift, gated * (p + 1) // shift, attn_step, 4)

            @pl.when(has_right)
            def _():
                helper_step([p])

            if p == early:

                @pl.when(has_left)
                def _():
                    local_copy(early).wait_send()

                @pl.when(lead)
                def _():
                    opened(0)

        @pl.when(has_right)
        def _():
            stat[0] = jnp.sum(jnp.transpose(dsq[...]).reshape(16, 8, SPAN), axis=0)
            stat[1] = jnp.sum(jnp.transpose(dnn[...]).reshape(16, 8, SPAN), axis=0)
            stat_right.start()

        attn_step([gated])

        @pl.when(has_right)
        def _():
            kv_copy(gated).wait_send()

        @pl.when(lead)
        def _():
            opened(1)

        attn_step([gated + 1])
        attn_step([gated + 2])

        @pl.when(has_left)
        def _():
            stat_right.wait_recv()

        extra_sq = jnp.transpose(jnp.broadcast_to(jnp.sum(statr[0], axis=0, keepdims=True), (DIM, SPAN)))
        extra_in = jnp.transpose(jnp.broadcast_to(jnp.sum(statr[1], axis=0, keepdims=True), (DIM, SPAN)))
    else:
        loop(0, HEADS, attn_step)
        extra_sq = extra_in = 0.0

    mean = jnp.broadcast_to(jnp.sum(ssq[...], axis=-1, keepdims=True), (SPAN, DIM)) + extra_sq
    inner = jnp.broadcast_to(jnp.sum(inn[...], axis=-1, keepdims=True), (SPAN, DIM)) + extra_in
    inv = 1.0 / jnp.sqrt(mean / features + 1e-05)
    coef = inner * inv**3 / features

    if shift:
        scal[0] = jnp.transpose(inv)[0:8]
        scal[1] = jnp.transpose(coef)[0:8]

        @pl.when(has_left)
        def _():
            scal_left.start()

    def da_step(hs):
        ds = []
        for h in hs:
            a = attn[:, cols(h)]
            g = y[:, cols(h)].astype(F32)
            ds.append((g * gain[h] * inv - a * coef).astype(BF16))
        for h, d in zip(hs, ds):
            da[:, cols(h)] = d
        return ds

    def gain_step(hs):
        rows_of = [
            jnp.sum(y[:, cols(h)].astype(F32) * attn[:, cols(h)] * inv, axis=0, keepdims=True) for h in hs
        ]
        for h, row in zip(hs, rows_of):
            gsum[h] = row

    def grad_all(hs):
        grad_step(hs)
        gain_step(hs)

    def held_step(hs):
        for h, m in [(h, dot(q[:, cols(h)], d, 0, 0)) for h, d in zip(hs, da_step(hs))]:
            qdo[h] = m

    def send_step(hs):
        held_step(hs)
        if not chain:

            @pl.when(has_left)
            def _():
                for h in hs:
                    back_copy(h).start()

    def grad_step(hs):
        ds = [da[:, cols(h)] for h in hs]
        scores = [dot(d, v[:, cols(h)], 1, 1) for h, d in zip(hs, ds)]
        ws = [jnp.where(causal, x, 0.0).astype(BF16) for x in scores]
        far = [dot(d, stb[h], 1, 1) for h, d in zip(hs, ds)]
        vs = [dot(intra[:, cols(h)], d, 0, 0) for h, d in zip(hs, ds)]
        qs = [dot(w, k[:, cols(h)], 1, 0) + f for h, w, f in zip(hs, ws, far)]
        kk = [dot(w, q[:, cols(h)], 0, 0) for h, w in zip(hs, ws)]
        for h, a, b, c in zip(hs, qs, kk, vs):
            gq[:, cols(h)] = a.astype(BF16)
            gkp[:, cols(h)] = b
            gvp[:, cols(h)] = c

    loop(0, plain, send_step, 2)

    def late_sends():
        @pl.when(has_right)
        def _():
            kv_copy(plain - 1).wait_send()
            for j in range(shift):
                kv_copy(plain + j).start()

    if shift:

        @pl.when(follow)
        def _():
            late_sends()
            opened(2)

    def late_step(hs):
        state_step(hs)
        da_step(hs)

    loop(0, plain, grad_all)

    if shift:
        for h in range(plain, HEADS):
            gsum[h] = jnp.zeros((1, DIM), F32)

        @pl.when(jnp.logical_not(has_left))
        def _():
            gain_step(list(range(plain, HEADS)))

        @pl.when(has_right)
        def _():
            scal_left.wait_recv()
            r_inv = jnp.transpose(jnp.broadcast_to(scalr[0, 0:1], (DIM, SPAN)))
            r_coef = jnp.transpose(jnp.broadcast_to(scalr[1, 0:1], (DIM, SPAN)))
            ds = []
            for j in range(shift):
                g, a = rstage[j, 1], rstage[j, 2]
                gsum[plain + j] = gsum[plain + j] + jnp.sum(g * a * r_inv, axis=0, keepdims=True)
                ds.append((g * gain[plain + j] * r_inv - a * r_coef).astype(BF16))
            for j, m in [(j, dot(rstage[j, 0].astype(BF16), d, 0, 0)) for j, d in enumerate(ds)]:
                bkr[plain + j] = m


    def ga_copy(o):
        to = lax.rem(mydp + o, ndp)
        return remote(
            gsum.at[pl.ds(to * hps, hps)], ga.at[o - 1], gas.at[o - 1], gar.at[o - 1], {"dp": to}
        )

    for o in range(1, ndp):
        ga_copy(o).start()

    if shift:

        @pl.when(lead)
        def _():
            pl.semaphore_wait(gate.at[2], 1)
            late_sends()

    for o in range(1, ndp):
        ga_copy(o).wait_recv()
    mine = gsum[pl.ds(mydp * hps, hps)]
    for o in range(1, ndp):
        mine = mine + ga[o - 1]
    gb[me] = mine

    def gb_send(o):
        return remote(gb.at[me], gb.at[me], gbs.at[o - 1], gbr.at[o - 1], {"ctx": lax.rem(me + o, n)})

    def gb_recv(o):
        source = lax.rem(me + n - o, n)
        return remote(gb.at[source], gb.at[source], gbs.at[o - 1], gbr.at[o - 1], {"ctx": lax.rem(me + o, n)})

    for o in range(1, n):
        gb_send(o).start()

    def finish(hs, backs):
        rounded = [back.astype(BF16) for back in backs]
        kk = [gkp[:, cols(h)] + dot(v[:, cols(h)], bb, 1, 1) for h, bb in zip(hs, rounded)]
        vs = [gvp[:, cols(h)] + dot(k[:, cols(h)], bb, 1, 0) for h, bb in zip(hs, rounded)]
        for h, a, b in zip(hs, kk, vs):
            gk[:, cols(h)] = a.astype(BF16)
            gv[:, cols(h)] = b.astype(BF16)

    if shift:

        def near_finish(hs):
            finish(hs, [jnp.where(from_right, bkr[h], 0.0) for h in hs])

        loop(plain, HEADS, late_step)
        loop(plain, HEADS, grad_step)
        loop(plain, HEADS, near_finish)

    def back_step(hs):
        @pl.when(has_right)
        def _():
            for h in hs:
                back_copy(h).wait_recv()

        backs = [jnp.where(from_right, bkr[h], 0.0) for h in hs]
        if chain:
            for h, back in zip(hs, backs):
                qdo[h] = qdo[h] + back

            @pl.when(has_left)
            def _():
                for h in hs:
                    back_copy(h).start()

        finish(hs, backs)

    loop(0, plain - 1, back_step, 2)
    for o in range(1, n):
        gb_recv(o).wait_recv()
    total = gb[0]
    for i in range(1, n):
        total = total + gb[i]
    gg_out[...] = total
    back_step([plain - 1])
    for o in range(1, n):
        gb_send(o).wait_send()
    for o in range(1, ndp):
        ga_copy(o).wait_send()

    @pl.when(has_right)
    def _():
        tag_right.wait_send()
        if shift:
            each(0, gated, lambda h: kv_copy(h).wait_send())
            kv_copy(gated + 1).wait_send()
            each(plain, HEADS, lambda h: kv_copy(h).wait_send())
            stat_right.wait_send()
        else:
            each(0, HEADS, lambda h: kv_copy(h).wait_send())

    @pl.when(has_left)
    def _():
        tag_left.wait_send()
        each(0, plain, lambda h: back_copy(h).wait_send())
        if shift:
            each(0, shift, lambda j: pair_copy(j).wait_send())
            for j in range(shift):
                if j != early:
                    local_copy(j).wait_send()
            scal_left.wait_send()


def writer(*refs):
    ins, outs, sem = refs[:4], refs[4:8], refs[8]
    copies = [pltpu.make_async_copy(a, b, sem.at[i]) for i, (a, b) in enumerate(zip(ins, outs))]
    for copy in copies:
        copy.start()
    for copy in copies:
        copy.wait()


def per_device(n, ndp, queries, keys, values, grad_normed, gain, doc_ids):
    batch, length, features = queries.shape
    flat = (length, features)
    hps = HEADS // ndp
    chain = n // 2 > 2
    shift = 0 if chain else SHIFT
    spare = max(shift, 1)
    vmem = pltpu.VMEM
    dma = pltpu.SemaphoreType.DMA
    hbm = pl.BlockSpec(memory_space=pltpu.HBM)
    near = pl.BlockSpec(memory_space=pltpu.VMEM)
    big = jax.ShapeDtypeStruct(flat, BF16)
    square = (HEADS, DIM, DIM)
    small = (2, 8, DIM)
    gq, gk, gv, gg = pl.pallas_call(
        functools.partial(kernel, n, ndp, chain, shift),
        out_shape=(big, big, big, jax.ShapeDtypeStruct((hps, 1, DIM), F32)),
        in_specs=[pl.BlockSpec(memory_space=pltpu.SMEM), hbm, hbm, hbm, hbm, hbm],
        out_specs=(near, near, near, near),
        scratch_shapes=[
            vmem((features,), BF16), vmem((HEADS, 1, DIM), F32),
            vmem(flat, BF16), vmem(flat, BF16), vmem(flat, BF16), vmem(flat, BF16),
            vmem(square, F32), vmem(square, F32),
            vmem(flat, BF16), vmem(flat, F32), vmem(flat, BF16), vmem(square, BF16),
            vmem(square, F32), vmem(square, F32),
            vmem(flat, F32), vmem(flat, F32),
            vmem((8, DIM), F32), vmem((8, DIM), F32), vmem((8, DIM), F32),
            vmem((SPAN, DIM), F32), vmem((SPAN, DIM), F32),
            vmem((HEADS, 1, DIM), F32), vmem((ndp - 1, hps, 1, DIM), F32), vmem((n, hps, 1, DIM), F32),
            vmem((spare, 3, SPAN, DIM), F32), vmem((spare, 3, SPAN, DIM), F32),
            vmem((SPAN, DIM), F32), vmem((SPAN, DIM), F32),
            vmem(small, F32), vmem(small, F32), vmem(small, F32), vmem(small, F32),
            dma((5,)),
            dma((HEADS,)), dma((HEADS,)), dma((HEADS,)), dma((HEADS,)),
            dma((2,)), dma((2,)),
            dma((ndp - 1,)), dma((ndp - 1,)), dma((n - 1,)), dma((n - 1,)),
            dma((spare, 2)), dma((spare, 2)), dma((2,)), dma((2,)),
            pltpu.SemaphoreType.REGULAR((3,)),
            pltpu.SemaphoreType.REGULAR,
        ],
        compiler_params=pltpu.CompilerParams(
            collective_id=0, has_side_effects=True, vmem_limit_bytes=40 << 20
        ),
        name="lin_attn_bwd",
    )(
        doc_ids,
        pltpu.with_memory_space_constraint(gain, pltpu.HBM),
        pltpu.with_memory_space_constraint(queries.reshape(flat), pltpu.HBM),
        pltpu.with_memory_space_constraint(keys.reshape(flat), pltpu.HBM),
        pltpu.with_memory_space_constraint(values.reshape(flat), pltpu.HBM),
        pltpu.with_memory_space_constraint(grad_normed.reshape(flat), pltpu.HBM),
    )
    anywhere = pl.BlockSpec(memory_space=pl.ANY)
    gq, gk, gv, gg = pl.pallas_call(
        writer,
        out_shape=(big, big, big, jax.ShapeDtypeStruct((hps, 1, DIM), F32)),
        in_specs=[anywhere] * 4,
        out_specs=(anywhere,) * 4,
        scratch_shapes=[dma((4,))],
        compiler_params=pltpu.CompilerParams(vmem_limit_bytes=1 << 20),
        name="write_out",
    )(gq, gk, gv, gg)
    whole = (batch, length, features)
    return gq.reshape(whole), gk.reshape(whole), gv.reshape(whole), gg.reshape(features // ndp)


def solution(mesh):
    rows = P(("group", "dp"), "ctx", None)
    return jax.shard_map(
        functools.partial(per_device, mesh.shape["ctx"], mesh.shape["dp"]),
        mesh=mesh,
        in_specs=(rows, rows, rows, rows, P(), P(("group", "dp"), "ctx")),
        out_specs=(rows, rows, rows, P(("group", "dp"))),
        check_vma=False,
    )
```

```python
import functools

import jax
import jax.numpy as jnp
from jax import lax
from jax.experimental import pallas as pl
from jax.experimental.pallas import tpu as pltpu
from jax.sharding import PartitionSpec as P

HEADS = 16
DIM = 128
SPAN = 128
SHIFTS = (2, 4)
HELD = 5
GROUP = 4
MESH = pl.DeviceIdType.MESH
F32 = jnp.float32
BF16 = jnp.bfloat16


def dot(a, b, ca, cb):
    return lax.dot_general(a, b, (((ca,), (cb,)), ((), ())), preferred_element_type=F32)


def kernel(
    n, ndp, chain, shifts, doc, gain_hbm, q_hbm, k_hbm, v_hbm, y_hbm,
    gq, gk, gv, gg_out,
    gain_in, gain, q, k, v, y, kvb, kvr, intra, attn, da, stb, qdo, bkr, gkp, gvp,
    tag, tagl, tagr, ssq, inn, gsum, ga, gb, stage, rstage, dsq, dnn, stat, statr, scal, scalr,
    in_sem, ks, kr, bs, br, ts, tr, gas, gar, gbs, gbr, ss, sr, ms, mr, gate, ready,
):
    me = lax.axis_index("ctx")
    mydp = lax.axis_index("dp")
    right, left = lax.rem(me + 1, n), lax.rem(me + n - 1, n)
    has_right, has_left = me < n - 1, me > 0
    lead = lax.rem(mydp, 2) == 0
    twin = mydp + 1 - 2 * lax.rem(mydp, 2)
    hps = HEADS // ndp
    features = HEADS * DIM

    edge, near_end = GROUP * DIM, (HEADS - GROUP) * DIM
    parts = [
        [(q_hbm, q, near_end, features), (y_hbm, y, near_end, features)],
        [(k_hbm, k, 0, edge), (v_hbm, v, 0, edge)],
        [(k_hbm, k, near_end, features), (v_hbm, v, near_end, features)],
        [(k_hbm, k, edge, near_end), (v_hbm, v, edge, near_end)],
        [(q_hbm, q, 0, near_end), (y_hbm, y, 0, near_end)],
    ]
    groups = []
    for part in parts:
        group = []
        for src, dst, first, last in part:
            i = 2 * len(groups) + len(group)
            group.append(
                pltpu.make_async_copy(src.at[:, first:last], dst.at[:, first:last], in_sem.at[i])
            )
        groups.append(group)
    groups[2].append(pltpu.make_async_copy(gain_hbm, gain_in, in_sem.at[10]))
    for load in groups[0] + groups[1]:
        load.start()

    def loaded(i):
        for load in groups[i]:
            load.wait()

    barrier = pltpu.get_barrier_semaphore()

    def greet(sem, axis, place, inside):
        @pl.when(inside)
        def _():
            pl.semaphore_signal(sem, inc=1, device_id={axis: place}, device_id_type=MESH)

    for o in range(1, n):
        greet(barrier, "ctx", lax.rem(me + o, n), me + o < n)
    greet(barrier, "ctx", left, has_left)
    for o in range(1, ndp):
        greet(barrier, "dp", lax.rem(mydp + o, ndp), mydp + o < ndp)

    for group in groups[2:]:
        for load in group:
            load.start()

    def cols(h):
        return pl.ds(pl.multiple_of(h * DIM, DIM), DIM)

    def loop(first, last, body, group=GROUP):
        whole = (last - first) // group

        def step(g, _):
            body([first + g * group + i for i in range(group)])
            return 0

        if whole == 1:
            step(0, 0)
        elif whole > 1:
            lax.fori_loop(0, whole, step, 0)
        if first + whole * group < last:
            body(list(range(first + whole * group, last)))

    def each(first, last, body):
        def step(h, _):
            body(h)
            return 0

        if last > first:
            lax.fori_loop(first, last, step, 0)

    def remote(src, dst, s, r, where):
        return pltpu.make_async_remote_copy(
            src_ref=src, dst_ref=dst, send_sem=s, recv_sem=r, device_id=where, device_id_type=MESH
        )

    to_right, to_left = {"ctx": right}, {"ctx": left}

    def kv_copy(h):
        return remote(kvb.at[h], kvr.at[h], ks.at[h], kr.at[h], to_right)

    def back_copy(h):
        return remote(qdo.at[h], bkr.at[h], bs.at[h], br.at[h], to_left)

    def pair_copy(j):
        return remote(stage.at[j, 0:2], rstage.at[j, 0:2], ss.at[j, 0], sr.at[j, 0], to_left)

    def local_copy(j):
        return remote(stage.at[j, 2], rstage.at[j, 2], ss.at[j, 1], sr.at[j, 1], to_left)

    def opened(i):
        pl.semaphore_signal(gate.at[i], inc=1, device_id={"dp": twin}, device_id_type=MESH)

    tag_right = remote(tag, tagl, ts.at[0], tr.at[0], to_right)
    tag_left = remote(tag, tagr, ts.at[1], tr.at[1], to_left)
    stat_right = remote(stat, statr, ms.at[0], mr.at[0], to_right)
    scal_left = remote(scal, scalr, ms.at[1], mr.at[1], to_left)

    own = (doc[0, 0] + 1).astype(F32)
    tag[...] = jnp.full((8, 128), own, F32)
    ssq[...] = jnp.zeros_like(ssq)
    inn[...] = jnp.zeros_like(inn)
    dsq[...] = jnp.zeros_like(dsq)
    dnn[...] = jnp.zeros_like(dnn)

    @pl.when(jnp.logical_not(has_left))
    def _():
        tagl[...] = jnp.full((8, 128), -1.0, F32)
        kvr[...] = jnp.zeros_like(kvr)
        statr[...] = jnp.zeros_like(statr)

    @pl.when(jnp.logical_not(has_right))
    def _():
        tagr[...] = jnp.full((8, 128), -1.0, F32)
        bkr[...] = jnp.zeros_like(bkr)

    rows = lax.broadcasted_iota(jnp.int32, (SPAN, SPAN), 0)
    lanes = lax.broadcasted_iota(jnp.int32, (SPAN, SPAN), 1)
    causal = rows >= lanes

    def kv_only(hs):
        for h, m in [(h, dot(k[:, cols(h)], v[:, cols(h)], 0, 0)) for h in hs]:
            kvb[h] = m

    def kv_step(hs):
        kv_only(hs)
        if not chain:

            @pl.when(has_right)
            def _():
                for h in hs:
                    kv_copy(h).start()

    def local_step(hs):
        scores = [dot(q[:, cols(h)], k[:, cols(h)], 1, 1) for h in hs]
        ws = [jnp.where(causal, x, 0.0).astype(BF16) for x in scores]
        outs = [dot(w, v[:, cols(h)], 1, 0) for h, w in zip(hs, ws)]
        for h, w, a in zip(hs, ws, outs):
            intra[:, cols(h)] = w
            attn[:, cols(h)] = a
        return outs

    def sums(terms):
        total = terms[0]
        for term in terms[1:]:
            total = total + term
        return total

    def norm_sums(hs, outs):
        ssq[...] += sums([a * a for a in outs])
        inn[...] += sums([y[:, cols(h)].astype(F32) * gain[h] * a for h, a in zip(hs, outs)])

    def run(role, shift):
        plain = HEADS - shift

        def wire(js, copy):
            @pl.when(has_left)
            def _():
                for j in js:
                    copy(j).start()

        loaded(0)
        for j in range(shift):
            stage[j, 0] = q[:, cols(plain + j)].astype(F32)
            stage[j, 1] = y[:, cols(plain + j)].astype(F32)
        loaded(1)
        kv_only([0])
        pl.semaphore_wait(barrier, me + jnp.where(has_right, 1, 0) + mydp)

        @pl.when(has_right)
        def _():
            tag_right.start()

        @pl.when(has_left)
        def _():
            tag_left.start()

        first_kv = kv_step if role == "lead" else kv_only
        if role == "lead":
            wire([0], pair_copy)

            @pl.when(has_right)
            def _():
                kv_copy(0).start()

        loop(1, GROUP, first_kv, GROUP - 1)
        loaded(2)
        for j in range(shift):
            h = plain + j
            stage[j, 2] = local_step([h])[0]
            if role == "lead":
                wire([j], local_copy)
                if j + 1 < shift:
                    wire([j + 1], pair_copy)

        for o in range(2, n):
            greet(ready, "ctx", lax.rem(me + n - o, n), me >= o)
        for o in range(1, ndp):
            greet(ready, "dp", lax.rem(mydp + ndp - o, ndp), mydp >= o)
        for h in range(HEADS):
            gain[h] = gain_in[h * DIM : (h + 1) * DIM].astype(F32).reshape(1, DIM)
        for h in range(plain, HEADS):
            norm_sums([h], [attn[:, cols(h)]])
        loaded(3)
        loop(GROUP, plain, first_kv)
        loop(plain, HEADS, kv_only)
        loaded(4)
        loop(0, plain, local_step)
        early = max(shift - 2, 0)

        later = jnp.where(has_right, n - 2 - me, 0) + ndp - 1 - mydp

        @pl.when(later > 0)
        def _():
            pl.semaphore_wait(ready, later)

        if role == "lead":

            @pl.when(has_left)
            def _():
                local_copy(early).wait_send()

            opened(0)
        elif role == "follow":
            pl.semaphore_wait(gate.at[0], 1)
            for j in range(shift):
                wire([j], pair_copy)
                wire([j], local_copy)
            pl.semaphore_wait(gate.at[1], 1)

            @pl.when(has_right)
            def _():
                each(0, plain, lambda h: kv_copy(h).start())


        @pl.when(has_left)
        def _():
            tag_right.wait_recv()

        @pl.when(has_right)
        def _():
            tag_left.wait_recv()

        from_left = jnp.broadcast_to(tagl[0:1, :] == tag[0:1, :], (DIM, DIM))
        from_right = jnp.broadcast_to(tagr[0:1, :] == tag[0:1, :], (DIM, DIM))

        def state_step(hs):
            @pl.when(has_left)
            def _():
                for h in hs:
                    kv_copy(h).wait_recv()

            states = [jnp.where(from_left, kvr[h], 0.0) for h in hs]
            if chain:
                for h, state in zip(hs, states):
                    kvb[h] = kvb[h] + state

                @pl.when(has_right)
                def _():
                    for h in hs:
                        kv_copy(h).start()

            rounded = [state.astype(BF16) for state in states]
            outs = [attn[:, cols(h)] + dot(q[:, cols(h)], sb, 1, 0) for h, sb in zip(hs, rounded)]
            for h, sb, a in zip(hs, rounded, outs):
                stb[h] = sb
                attn[:, cols(h)] = a
            return outs

        def attn_step(hs):
            norm_sums(hs, state_step(hs))

        def helper_step(js):
            for j in js:
                pair_copy(j).wait_recv()
                local_copy(j).wait_recv()
            kbs = [jnp.where(from_right, kvb[plain + j], 0.0).astype(BF16) for j in js]
            xs = [dot(rstage[j, 0].astype(BF16), kb, 1, 0) for j, kb in zip(js, kbs)]
            olds = [rstage[j, 2] for j in js]
            dsq[...] += sums([(2.0 * a + x) * x for a, x in zip(olds, xs)])
            dnn[...] += sums([rstage[j, 1] * gain[plain + j] * x for j, x in zip(js, xs)])
            for j, a, x in zip(js, olds, xs):
                rstage[j, 2] = a + x

        gated = plain - 5
        if shift:
            for p in range(shift):
                loop(gated * p // shift, gated * (p + 1) // shift, attn_step, 4)

                @pl.when(has_right)
                def _():
                    helper_step([p])

            @pl.when(has_right)
            def _():
                stat[0] = jnp.sum(jnp.transpose(dsq[...]).reshape(16, 8, SPAN), axis=0)
                stat[1] = jnp.sum(jnp.transpose(dnn[...]).reshape(16, 8, SPAN), axis=0)
                stat_right.start()

            attn_step([gated, gated + 1])
            if role == "lead":

                @pl.when(has_right)
                def _():
                    kv_copy(gated + 2).wait_send()

                opened(1)

            attn_step([gated + 2])
            attn_step([gated + 3])
            attn_step([gated + 4])

            @pl.when(has_left)
            def _():
                stat_right.wait_recv()

            extra_sq = jnp.transpose(jnp.broadcast_to(jnp.sum(statr[0], axis=0, keepdims=True), (DIM, SPAN)))
            extra_in = jnp.transpose(jnp.broadcast_to(jnp.sum(statr[1], axis=0, keepdims=True), (DIM, SPAN)))
        else:
            loop(0, HEADS, attn_step)
            extra_sq = extra_in = 0.0

        mean = jnp.broadcast_to(jnp.sum(ssq[...], axis=-1, keepdims=True), (SPAN, DIM)) + extra_sq
        inner = jnp.broadcast_to(jnp.sum(inn[...], axis=-1, keepdims=True), (SPAN, DIM)) + extra_in
        inv = 1.0 / jnp.sqrt(mean / features + 1e-05)
        coef = inner * inv**3 / features

        if shift:
            scal[0] = jnp.transpose(inv)[0:8]
            scal[1] = jnp.transpose(coef)[0:8]

            @pl.when(has_left)
            def _():
                scal_left.start()

        def da_step(hs):
            ds = []
            for h in hs:
                a = attn[:, cols(h)]
                g = y[:, cols(h)].astype(F32)
                ds.append((g * gain[h] * inv - a * coef).astype(BF16))
            for h, d in zip(hs, ds):
                da[:, cols(h)] = d
            return ds

        def gain_step(hs):
            rows_of = [
                jnp.sum(y[:, cols(h)].astype(F32) * attn[:, cols(h)] * inv, axis=0, keepdims=True) for h in hs
            ]
            for h, row in zip(hs, rows_of):
                gsum[h] = row

        def grad_all(hs):
            grad_step(hs)
            gain_step(hs)

        def held_step(hs):
            for h, m in [(h, dot(q[:, cols(h)], d, 0, 0)) for h, d in zip(hs, da_step(hs))]:
                qdo[h] = m

        def back_sends(first, last):
            @pl.when(has_left)
            def _():
                for h in range(first, last):
                    back_copy(h).start()

        def send_step(hs):
            held_step(hs)
            if role != "chain":

                @pl.when(has_left)
                def _():
                    for h in hs:
                        back_copy(h).start()

        def grad_step(hs):
            ds = [da[:, cols(h)] for h in hs]
            scores = [dot(d, v[:, cols(h)], 1, 1) for h, d in zip(hs, ds)]
            ws = [jnp.where(causal, x, 0.0).astype(BF16) for x in scores]
            far = [dot(d, stb[h], 1, 1) for h, d in zip(hs, ds)]
            vs = [dot(intra[:, cols(h)], d, 0, 0) for h, d in zip(hs, ds)]
            qs = [dot(w, k[:, cols(h)], 1, 0) + f for h, w, f in zip(hs, ws, far)]
            kk = [dot(w, q[:, cols(h)], 0, 0) for h, w in zip(hs, ws)]
            for h, a, b, c in zip(hs, qs, kk, vs):
                gq[:, cols(h)] = a.astype(BF16)
                gkp[:, cols(h)] = b
                gvp[:, cols(h)] = c

        def ga_copy(o):
            to = lax.rem(mydp + o, ndp)
            return remote(
                gsum.at[pl.ds(to * hps, hps)], ga.at[o - 1], gas.at[o - 1], gar.at[o - 1], {"dp": to}
            )

        def gb_send(o):
            return remote(gb.at[me], gb.at[me], gbs.at[o - 1], gbr.at[o - 1], {"ctx": lax.rem(me + o, n)})

        def gb_recv(o):
            source = lax.rem(me + n - o, n)
            return remote(gb.at[source], gb.at[source], gbs.at[o - 1], gbr.at[o - 1], {"ctx": lax.rem(me + o, n)})

        def finish(hs, backs):
            rounded = [back.astype(BF16) for back in backs]
            kk = [gkp[:, cols(h)] + dot(v[:, cols(h)], bb, 1, 1) for h, bb in zip(hs, rounded)]
            vs = [gvp[:, cols(h)] + dot(k[:, cols(h)], bb, 1, 0) for h, bb in zip(hs, rounded)]
            for h, a, b in zip(hs, kk, vs):
                gk[:, cols(h)] = a.astype(BF16)
                gv[:, cols(h)] = b.astype(BF16)

        def back_step(hs):
            @pl.when(has_right)
            def _():
                for h in hs:
                    back_copy(h).wait_recv()

            backs = [jnp.where(from_right, bkr[h], 0.0) for h in hs]
            if chain:
                for h, back in zip(hs, backs):
                    qdo[h] = qdo[h] + back

                @pl.when(has_left)
                def _():
                    for h in hs:
                        back_copy(h).start()

            finish(hs, backs)

        def late_step(hs):
            state_step(hs)
            da_step(hs)

        def late_sends():
            @pl.when(has_right)
            def _():
                for j in range(shift):
                    kv_copy(plain + j).start()

        def near_step():
                for h in range(plain, HEADS):
                    gsum[h] = jnp.zeros((1, DIM), F32)

                @pl.when(jnp.logical_not(has_left))
                def _():
                    gain_step(list(range(plain, HEADS)))

                @pl.when(has_right)
                def _():
                    scal_left.wait_recv()
                    r_inv = jnp.transpose(jnp.broadcast_to(scalr[0, 0:1], (DIM, SPAN)))
                    r_coef = jnp.transpose(jnp.broadcast_to(scalr[1, 0:1], (DIM, SPAN)))
                    ds = []
                    for j in range(shift):
                        g, a = rstage[j, 1], rstage[j, 2]
                        gsum[plain + j] = gsum[plain + j] + jnp.sum(g * a * r_inv, axis=0, keepdims=True)
                        ds.append((g * gain[plain + j] * r_inv - a * r_coef).astype(BF16))
                    for j, m in [(j, dot(rstage[j, 0].astype(BF16), d, 0, 0)) for j, d in enumerate(ds)]:
                        bkr[plain + j] = m


        def ga_sends():
            for o in range(1, ndp):
                ga_copy(o).start()

        def gb_sends():
            for o in range(1, ndp):
                ga_copy(o).wait_recv()
            mine = gsum[pl.ds(mydp * hps, hps)]
            for o in range(1, ndp):
                mine = mine + ga[o - 1]
            gb[me] = mine
            for o in range(1, n):
                gb_send(o).start()

        def gb_total():
            for o in range(1, n):
                gb_recv(o).wait_recv()
            total = gb[0]
            for i in range(1, n):
                total = total + gb[i]
            gg_out[...] = total

        def near_finish(hs):
            finish(hs, [jnp.where(from_right, bkr[h], 0.0) for h in hs])

        def late_grads():
            loop(plain, HEADS, late_step)
            loop(plain, HEADS, grad_step)
            loop(plain, HEADS, near_finish)

        if role == "lead":
            send_step([0])
            loop(1, plain, send_step, 2)
            loop(0, plain, grad_all)
            near_step()
            ga_sends()
            loop(0, plain, back_step, 2)
            late_sends()
            gb_sends()
            late_grads()
            gb_total()
        elif role == "follow":
            sent = plain - HELD
            send_step([0])
            loop(1, sent, send_step, 2)
            loop(sent, plain, held_step, HELD)
            loop(0, plain, gain_step)
            near_step()
            ga_sends()
            late_sends()
            loop(0, GROUP, grad_step)
            gb_sends()
            back_sends(sent, plain)
            loop(GROUP, plain, grad_step)
            late_grads()
            loop(0, plain - 1, back_step, 2)
            gb_total()
            back_step([plain - 1])
        else:
            loop(0, plain, held_step, 2)
            loop(0, plain, grad_all)
            ga_sends()
            gb_sends()
            loop(0, plain, back_step, 2)
            gb_total()

        for o in range(1, n):
            gb_send(o).wait_send()
        for o in range(1, ndp):
            ga_copy(o).wait_send()

        @pl.when(has_right)
        def _():
            tag_right.wait_send()
            if role == "lead":
                each(0, gated + 2, lambda h: kv_copy(h).wait_send())
                each(gated + 3, HEADS, lambda h: kv_copy(h).wait_send())
            else:
                each(0, HEADS, lambda h: kv_copy(h).wait_send())
            if shift:
                stat_right.wait_send()

        @pl.when(has_left)
        def _():
            tag_left.wait_send()
            each(0, plain, lambda h: back_copy(h).wait_send())
            if shift:
                each(0, shift, lambda j: pair_copy(j).wait_send())
                for j in range(shift):
                    if role != "lead" or j != early:
                        local_copy(j).wait_send()
                scal_left.wait_send()

    if chain:
        run("chain", 0)
    else:

        @pl.when(lead)
        def _():
            run("lead", shifts[0])

        @pl.when(jnp.logical_not(lead))
        def _():
            run("follow", shifts[1])


def writer(*refs):
    ins, outs, sem = refs[:4], refs[4:8], refs[8]
    copies = [pltpu.make_async_copy(a, b, sem.at[i]) for i, (a, b) in enumerate(zip(ins, outs))]
    for copy in copies:
        copy.start()
    for copy in copies:
        copy.wait()


def per_device(n, ndp, queries, keys, values, grad_normed, gain, doc_ids):
    batch, length, features = queries.shape
    flat = (length, features)
    hps = HEADS // ndp
    chain = n // 2 > 2
    shifts = (0,) if chain else SHIFTS
    spare = max(shifts + (1,))
    vmem = pltpu.VMEM
    dma = pltpu.SemaphoreType.DMA
    hbm = pl.BlockSpec(memory_space=pltpu.HBM)
    near = pl.BlockSpec(memory_space=pltpu.VMEM)
    big = jax.ShapeDtypeStruct(flat, BF16)
    square = (HEADS, DIM, DIM)
    small = (2, 8, DIM)
    gq, gk, gv, gg = pl.pallas_call(
        functools.partial(kernel, n, ndp, chain, shifts),
        out_shape=(big, big, big, jax.ShapeDtypeStruct((hps, 1, DIM), F32)),
        in_specs=[pl.BlockSpec(memory_space=pltpu.SMEM), hbm, hbm, hbm, hbm, hbm],
        out_specs=(near, near, near, near),
        scratch_shapes=[
            vmem((features,), BF16), vmem((HEADS, 1, DIM), F32),
            vmem(flat, BF16), vmem(flat, BF16), vmem(flat, BF16), vmem(flat, BF16),
            vmem(square, F32), vmem(square, F32),
            vmem(flat, BF16), vmem(flat, F32), vmem(flat, BF16), vmem(square, BF16),
            vmem(square, F32), vmem(square, F32),
            vmem(flat, F32), vmem(flat, F32),
            vmem((8, DIM), F32), vmem((8, DIM), F32), vmem((8, DIM), F32),
            vmem((SPAN, DIM), F32), vmem((SPAN, DIM), F32),
            vmem((HEADS, 1, DIM), F32), vmem((ndp - 1, hps, 1, DIM), F32), vmem((n, hps, 1, DIM), F32),
            vmem((spare, 3, SPAN, DIM), F32), vmem((spare, 3, SPAN, DIM), F32),
            vmem((SPAN, DIM), F32), vmem((SPAN, DIM), F32),
            vmem(small, F32), vmem(small, F32), vmem(small, F32), vmem(small, F32),
            dma((11,)),
            dma((HEADS,)), dma((HEADS,)), dma((HEADS,)), dma((HEADS,)),
            dma((2,)), dma((2,)),
            dma((ndp - 1,)), dma((ndp - 1,)), dma((n - 1,)), dma((n - 1,)),
            dma((spare, 2)), dma((spare, 2)), dma((2,)), dma((2,)),
            pltpu.SemaphoreType.REGULAR((2,)),
            pltpu.SemaphoreType.REGULAR,
        ],
        compiler_params=pltpu.CompilerParams(
            collective_id=0, has_side_effects=True, vmem_limit_bytes=40 << 20
        ),
        name="lin_attn_bwd",
    )(
        doc_ids,
        pltpu.with_memory_space_constraint(gain, pltpu.HBM),
        pltpu.with_memory_space_constraint(queries.reshape(flat), pltpu.HBM),
        pltpu.with_memory_space_constraint(keys.reshape(flat), pltpu.HBM),
        pltpu.with_memory_space_constraint(values.reshape(flat), pltpu.HBM),
        pltpu.with_memory_space_constraint(grad_normed.reshape(flat), pltpu.HBM),
    )
    anywhere = pl.BlockSpec(memory_space=pl.ANY)
    gq, gk, gv, gg = pl.pallas_call(
        writer,
        out_shape=(big, big, big, jax.ShapeDtypeStruct((hps, 1, DIM), F32)),
        in_specs=[anywhere] * 4,
        out_specs=(anywhere,) * 4,
        scratch_shapes=[dma((4,))],
        compiler_params=pltpu.CompilerParams(vmem_limit_bytes=1 << 20),
        name="write_out",
    )(gq, gk, gv, gg)
    whole = (batch, length, features)
    return gq.reshape(whole), gk.reshape(whole), gv.reshape(whole), gg.reshape(features // ndp)


def solution(mesh):
    rows = P(("group", "dp"), "ctx", None)
    return jax.shard_map(
        functools.partial(per_device, mesh.shape["ctx"], mesh.shape["dp"]),
        mesh=mesh,
        in_specs=(rows, rows, rows, rows, P(), P(("group", "dp"), "ctx")),
        out_specs=(rows, rows, rows, P(("group", "dp"))),
        check_vma=False,
    )
```

```python
import functools

import jax
import jax.numpy as jnp
from jax import lax
from jax.experimental import pallas as pl
from jax.experimental.pallas import tpu as pltpu
from jax.sharding import PartitionSpec as P

HEADS = 16
DIM = 128
SPAN = 128
SHIFTS = (2, 4)
HELD = 5
GROUP = 4
MESH = pl.DeviceIdType.MESH
F32 = jnp.float32
BF16 = jnp.bfloat16


def dot(a, b, ca, cb):
    return lax.dot_general(a, b, (((ca,), (cb,)), ((), ())), preferred_element_type=F32)


def kernel(
    n, ndp, chain, shifts, doc, gain_hbm, q_hbm, k_hbm, v_hbm, y_hbm,
    gq, gk, gv, gg_out,
    gain_in, gain, q, k, v, y, kvb, kvr, intra, attn, da, stb, qdo, bkr, gkp, gvp,
    tag, tagl, tagr, ssq, inn, gsum, ga, gb, stage, rstage, dsq, dnn, stat, statr, scal, scalr,
    in_sem, ks, kr, bs, br, ts, tr, gas, gar, gbs, gbr, ss, sr, ms, mr, gate, ready,
):
    me = lax.axis_index("ctx")
    mydp = lax.axis_index("dp")
    right, left = lax.rem(me + 1, n), lax.rem(me + n - 1, n)
    has_right, has_left = me < n - 1, me > 0
    lead = lax.rem(mydp, 2) == 0
    twin = mydp + 1 - 2 * lax.rem(mydp, 2)
    hps = HEADS // ndp
    features = HEADS * DIM

    edge, near_end = GROUP * DIM, (HEADS - GROUP) * DIM
    parts = [
        [(q_hbm, q, near_end, features), (y_hbm, y, near_end, features)],
        [(k_hbm, k, 0, edge), (v_hbm, v, 0, edge)],
        [(k_hbm, k, near_end, features), (v_hbm, v, near_end, features)],
        [(k_hbm, k, edge, near_end), (v_hbm, v, edge, near_end)],
        [(q_hbm, q, 0, near_end), (y_hbm, y, 0, near_end)],
    ]
    groups = []
    for part in parts:
        group = []
        for src, dst, first, last in part:
            i = 2 * len(groups) + len(group)
            group.append(
                pltpu.make_async_copy(src.at[:, first:last], dst.at[:, first:last], in_sem.at[i])
            )
        groups.append(group)
    groups[2].append(pltpu.make_async_copy(gain_hbm, gain_in, in_sem.at[10]))
    for load in groups[0] + groups[1]:
        load.start()

    def loaded(i):
        for load in groups[i]:
            load.wait()

    barrier = pltpu.get_barrier_semaphore()

    def greet(sem, axis, place, inside):
        @pl.when(inside)
        def _():
            pl.semaphore_signal(sem, inc=1, device_id={axis: place}, device_id_type=MESH)

    for o in range(1, n):
        greet(barrier, "ctx", lax.rem(me + o, n), me + o < n)
    greet(barrier, "ctx", left, has_left)
    for o in range(1, ndp):
        greet(barrier, "dp", lax.rem(mydp + o, ndp), mydp + o < ndp)

    for group in groups[2:]:
        for load in group:
            load.start()

    def cols(h):
        return pl.ds(pl.multiple_of(h * DIM, DIM), DIM)

    def loop(first, last, body, group=GROUP):
        whole = (last - first) // group

        def step(g, _):
            body([first + g * group + i for i in range(group)])
            return 0

        if whole == 1:
            step(0, 0)
        elif whole > 1:
            lax.fori_loop(0, whole, step, 0)
        if first + whole * group < last:
            body(list(range(first + whole * group, last)))

    def each(first, last, body):
        def step(h, _):
            body(h)
            return 0

        if last > first:
            lax.fori_loop(first, last, step, 0)

    def remote(src, dst, s, r, where):
        return pltpu.make_async_remote_copy(
            src_ref=src, dst_ref=dst, send_sem=s, recv_sem=r, device_id=where, device_id_type=MESH
        )

    to_right, to_left = {"ctx": right}, {"ctx": left}

    def kv_copy(h):
        return remote(kvb.at[h], kvr.at[h], ks.at[h], kr.at[h], to_right)

    def back_copy(h):
        return remote(qdo.at[h], bkr.at[h], bs.at[h], br.at[h], to_left)

    def pair_copy(j):
        return remote(stage.at[j, 0:2], rstage.at[j, 0:2], ss.at[j, 0], sr.at[j, 0], to_left)

    def local_copy(j):
        return remote(stage.at[j, 2], rstage.at[j, 2], ss.at[j, 1], sr.at[j, 1], to_left)

    tag_right = remote(tag, tagl, ts.at[0], tr.at[0], to_right)
    tag_left = remote(tag, tagr, ts.at[1], tr.at[1], to_left)
    stat_right = remote(stat, statr, ms.at[0], mr.at[0], to_right)
    scal_left = remote(scal, scalr, ms.at[1], mr.at[1], to_left)

    own = (doc[0, 0] + 1).astype(F32)
    tag[...] = jnp.full((8, 128), own, F32)
    ssq[...] = jnp.zeros_like(ssq)
    inn[...] = jnp.zeros_like(inn)
    dsq[...] = jnp.zeros_like(dsq)
    dnn[...] = jnp.zeros_like(dnn)

    @pl.when(jnp.logical_not(has_left))
    def _():
        tagl[...] = jnp.full((8, 128), -1.0, F32)
        kvr[...] = jnp.zeros_like(kvr)
        statr[...] = jnp.zeros_like(statr)

    @pl.when(jnp.logical_not(has_right))
    def _():
        tagr[...] = jnp.full((8, 128), -1.0, F32)
        bkr[...] = jnp.zeros_like(bkr)

    rows = lax.broadcasted_iota(jnp.int32, (SPAN, SPAN), 0)
    lanes = lax.broadcasted_iota(jnp.int32, (SPAN, SPAN), 1)
    causal = rows >= lanes

    def kv_only(hs):
        for h, m in [(h, dot(k[:, cols(h)], v[:, cols(h)], 0, 0)) for h in hs]:
            kvb[h] = m

    def kv_step(hs):
        kv_only(hs)
        if not chain:

            @pl.when(has_right)
            def _():
                for h in hs:
                    kv_copy(h).start()

    def local_step(hs):
        scores = [dot(q[:, cols(h)], k[:, cols(h)], 1, 1) for h in hs]
        ws = [jnp.where(causal, x, 0.0).astype(BF16) for x in scores]
        outs = [dot(w, v[:, cols(h)], 1, 0) for h, w in zip(hs, ws)]
        for h, w, a in zip(hs, ws, outs):
            intra[:, cols(h)] = w
            attn[:, cols(h)] = a
        return outs

    def sums(terms):
        total = terms[0]
        for term in terms[1:]:
            total = total + term
        return total

    def norm_sums(hs, outs):
        ssq[...] += sums([a * a for a in outs])
        inn[...] += sums([y[:, cols(h)].astype(F32) * gain[h] * a for h, a in zip(hs, outs)])

    def run(role, shift):
        plain = HEADS - shift

        def wire(js, copy):
            @pl.when(has_left)
            def _():
                for j in js:
                    copy(j).start()

        loaded(0)
        for j in range(shift):
            stage[j, 0] = q[:, cols(plain + j)].astype(F32)
            stage[j, 1] = y[:, cols(plain + j)].astype(F32)
        loaded(1)
        kv_only([0])
        pl.semaphore_wait(barrier, me + jnp.where(has_right, 1, 0) + mydp)

        @pl.when(has_right)
        def _():
            tag_right.start()

        @pl.when(has_left)
        def _():
            tag_left.start()

        first_kv = kv_step if role == "lead" else kv_only
        if role == "lead":
            wire([0], pair_copy)

            @pl.when(has_right)
            def _():
                kv_copy(0).start()

        loop(1, GROUP, first_kv, GROUP - 1)
        loaded(2)
        for j in range(shift):
            h = plain + j
            stage[j, 2] = local_step([h])[0]
            if role == "lead":
                wire([j], local_copy)
                if j + 1 < shift:
                    wire([j + 1], pair_copy)

        for o in range(2, n):
            greet(ready, "ctx", lax.rem(me + n - o, n), me >= o)
        for o in range(1, ndp):
            greet(ready, "dp", lax.rem(mydp + ndp - o, ndp), mydp >= o)
        for h in range(HEADS):
            gain[h] = gain_in[h * DIM : (h + 1) * DIM].astype(F32).reshape(1, DIM)
        for h in range(plain, HEADS):
            norm_sums([h], [attn[:, cols(h)]])
        loaded(3)
        loop(GROUP, plain, first_kv)
        loop(plain, HEADS, kv_only)
        loaded(4)
        loop(0, plain, local_step)

        later = jnp.where(has_right, n - 2 - me, 0) + ndp - 1 - mydp

        @pl.when(later > 0)
        def _():
            pl.semaphore_wait(ready, later)

        if role == "follow":
            for j in range(shift):
                wire([j], pair_copy)
                wire([j], local_copy)
            pl.semaphore_wait(gate, 1)

            @pl.when(has_right)
            def _():
                each(0, plain, lambda h: kv_copy(h).start())


        @pl.when(has_left)
        def _():
            tag_right.wait_recv()

        @pl.when(has_right)
        def _():
            tag_left.wait_recv()

        from_left = jnp.broadcast_to(tagl[0:1, :] == tag[0:1, :], (DIM, DIM))
        from_right = jnp.broadcast_to(tagr[0:1, :] == tag[0:1, :], (DIM, DIM))

        def state_step(hs):
            @pl.when(has_left)
            def _():
                for h in hs:
                    kv_copy(h).wait_recv()

            states = [jnp.where(from_left, kvr[h], 0.0) for h in hs]
            if chain:
                for h, state in zip(hs, states):
                    kvb[h] = kvb[h] + state

                @pl.when(has_right)
                def _():
                    for h in hs:
                        kv_copy(h).start()

            rounded = [state.astype(BF16) for state in states]
            outs = [attn[:, cols(h)] + dot(q[:, cols(h)], sb, 1, 0) for h, sb in zip(hs, rounded)]
            for h, sb, a in zip(hs, rounded, outs):
                stb[h] = sb
                attn[:, cols(h)] = a
            return outs

        def attn_step(hs):
            norm_sums(hs, state_step(hs))

        def helper_step(js):
            for j in js:
                pair_copy(j).wait_recv()
                local_copy(j).wait_recv()
            kbs = [jnp.where(from_right, kvb[plain + j], 0.0).astype(BF16) for j in js]
            xs = [dot(rstage[j, 0].astype(BF16), kb, 1, 0) for j, kb in zip(js, kbs)]
            olds = [rstage[j, 2] for j in js]
            dsq[...] += sums([(2.0 * a + x) * x for a, x in zip(olds, xs)])
            dnn[...] += sums([rstage[j, 1] * gain[plain + j] * x for j, x in zip(js, xs)])
            for j, a, x in zip(js, olds, xs):
                rstage[j, 2] = a + x

        gated = plain - 5
        if shift:
            for p in range(shift):
                loop(gated * p // shift, gated * (p + 1) // shift, attn_step, 4)

                @pl.when(has_right)
                def _():
                    helper_step([p])

            @pl.when(has_right)
            def _():
                stat[0] = jnp.sum(jnp.transpose(dsq[...]).reshape(16, 8, SPAN), axis=0)
                stat[1] = jnp.sum(jnp.transpose(dnn[...]).reshape(16, 8, SPAN), axis=0)
                stat_right.start()

            attn_step([gated, gated + 1])
            if role == "lead":

                @pl.when(has_right)
                def _():
                    kv_copy(gated + 2).wait_send()

                pl.semaphore_signal(gate, inc=1, device_id={"dp": twin}, device_id_type=MESH)

            attn_step([gated + 2])
            attn_step([gated + 3])
            attn_step([gated + 4])

            @pl.when(has_left)
            def _():
                stat_right.wait_recv()

            extra_sq = jnp.transpose(jnp.broadcast_to(jnp.sum(statr[0], axis=0, keepdims=True), (DIM, SPAN)))
            extra_in = jnp.transpose(jnp.broadcast_to(jnp.sum(statr[1], axis=0, keepdims=True), (DIM, SPAN)))
        else:
            loop(0, HEADS, attn_step)
            extra_sq = extra_in = 0.0

        mean = jnp.broadcast_to(jnp.sum(ssq[...], axis=-1, keepdims=True), (SPAN, DIM)) + extra_sq
        inner = jnp.broadcast_to(jnp.sum(inn[...], axis=-1, keepdims=True), (SPAN, DIM)) + extra_in
        inv = 1.0 / jnp.sqrt(mean / features + 1e-05)
        coef = inner * inv**3 / features

        if shift:
            scal[0] = jnp.transpose(inv)[0:8]
            scal[1] = jnp.transpose(coef)[0:8]

            @pl.when(has_left)
            def _():
                scal_left.start()

        def da_step(hs):
            ds = []
            for h in hs:
                a = attn[:, cols(h)]
                g = y[:, cols(h)].astype(F32)
                ds.append((g * gain[h] * inv - a * coef).astype(BF16))
            for h, d in zip(hs, ds):
                da[:, cols(h)] = d
            return ds

        def gain_step(hs):
            rows_of = [
                jnp.sum(y[:, cols(h)].astype(F32) * attn[:, cols(h)] * inv, axis=0, keepdims=True) for h in hs
            ]
            for h, row in zip(hs, rows_of):
                gsum[h] = row

        def grad_all(hs):
            grad_step(hs)
            gain_step(hs)

        def held_step(hs):
            for h, m in [(h, dot(q[:, cols(h)], d, 0, 0)) for h, d in zip(hs, da_step(hs))]:
                qdo[h] = m

        def back_sends(first, last):
            @pl.when(has_left)
            def _():
                for h in range(first, last):
                    back_copy(h).start()

        def send_step(hs):
            held_step(hs)
            if role != "chain":

                @pl.when(has_left)
                def _():
                    for h in hs:
                        back_copy(h).start()

        def grad_step(hs):
            ds = [da[:, cols(h)] for h in hs]
            scores = [dot(d, v[:, cols(h)], 1, 1) for h, d in zip(hs, ds)]
            ws = [jnp.where(causal, x, 0.0).astype(BF16) for x in scores]
            far = [dot(d, stb[h], 1, 1) for h, d in zip(hs, ds)]
            vs = [dot(intra[:, cols(h)], d, 0, 0) for h, d in zip(hs, ds)]
            qs = [dot(w, k[:, cols(h)], 1, 0) + f for h, w, f in zip(hs, ws, far)]
            kk = [dot(w, q[:, cols(h)], 0, 0) for h, w in zip(hs, ws)]
            for h, a, b, c in zip(hs, qs, kk, vs):
                gq[:, cols(h)] = a.astype(BF16)
                gkp[:, cols(h)] = b
                gvp[:, cols(h)] = c

        def ga_copy(o):
            to = lax.rem(mydp + o, ndp)
            return remote(
                gsum.at[pl.ds(to * hps, hps)], ga.at[o - 1], gas.at[o - 1], gar.at[o - 1], {"dp": to}
            )

        def gb_send(o):
            return remote(gb.at[me], gb.at[me], gbs.at[o - 1], gbr.at[o - 1], {"ctx": lax.rem(me + o, n)})

        def gb_recv(o):
            source = lax.rem(me + n - o, n)
            return remote(gb.at[source], gb.at[source], gbs.at[o - 1], gbr.at[o - 1], {"ctx": lax.rem(me + o, n)})

        def finish(hs, backs):
            rounded = [back.astype(BF16) for back in backs]
            kk = [gkp[:, cols(h)] + dot(v[:, cols(h)], bb, 1, 1) for h, bb in zip(hs, rounded)]
            vs = [gvp[:, cols(h)] + dot(k[:, cols(h)], bb, 1, 0) for h, bb in zip(hs, rounded)]
            for h, a, b in zip(hs, kk, vs):
                gk[:, cols(h)] = a.astype(BF16)
                gv[:, cols(h)] = b.astype(BF16)

        def back_step(hs):
            @pl.when(has_right)
            def _():
                for h in hs:
                    back_copy(h).wait_recv()

            backs = [jnp.where(from_right, bkr[h], 0.0) for h in hs]
            if chain:
                for h, back in zip(hs, backs):
                    qdo[h] = qdo[h] + back

                @pl.when(has_left)
                def _():
                    for h in hs:
                        back_copy(h).start()

            finish(hs, backs)

        def late_step(hs):
            state_step(hs)
            da_step(hs)

        def late_sends():
            @pl.when(has_right)
            def _():
                for j in range(shift):
                    kv_copy(plain + j).start()

        def near_step():
                for h in range(plain, HEADS):
                    gsum[h] = jnp.zeros((1, DIM), F32)

                @pl.when(jnp.logical_not(has_left))
                def _():
                    gain_step(list(range(plain, HEADS)))

                @pl.when(has_right)
                def _():
                    scal_left.wait_recv()
                    r_inv = jnp.transpose(jnp.broadcast_to(scalr[0, 0:1], (DIM, SPAN)))
                    r_coef = jnp.transpose(jnp.broadcast_to(scalr[1, 0:1], (DIM, SPAN)))
                    ds = []
                    for j in range(shift):
                        g, a = rstage[j, 1], rstage[j, 2]
                        gsum[plain + j] = gsum[plain + j] + jnp.sum(g * a * r_inv, axis=0, keepdims=True)
                        ds.append((g * gain[plain + j] * r_inv - a * r_coef).astype(BF16))
                    for j, m in [(j, dot(rstage[j, 0].astype(BF16), d, 0, 0)) for j, d in enumerate(ds)]:
                        bkr[plain + j] = m


        def ga_sends():
            for o in range(1, ndp):
                ga_copy(o).start()

        def gb_sends():
            for o in range(1, ndp):
                ga_copy(o).wait_recv()
            mine = gsum[pl.ds(mydp * hps, hps)]
            for o in range(1, ndp):
                mine = mine + ga[o - 1]
            gb[me] = mine
            for o in range(1, n):
                gb_send(o).start()

        def gb_total():
            for o in range(1, n):
                gb_recv(o).wait_recv()
            total = gb[0]
            for i in range(1, n):
                total = total + gb[i]
            gg_out[...] = total

        def near_finish(hs):
            finish(hs, [jnp.where(from_right, bkr[h], 0.0) for h in hs])

        def late_grads():
            loop(plain, HEADS, late_step)
            loop(plain, HEADS, grad_step)
            loop(plain, HEADS, near_finish)

        if role == "lead":
            send_step([0])
            loop(1, plain, send_step, 2)
            loop(0, plain, grad_all)
            near_step()
            ga_sends()
            loop(0, plain, back_step, 2)
            late_sends()
            gb_sends()
            late_grads()
            gb_total()
        elif role == "follow":
            sent = plain - HELD
            send_step([0])
            loop(1, sent, send_step, 2)
            loop(sent, plain, held_step, HELD)
            loop(0, plain, gain_step)
            near_step()
            ga_sends()
            late_sends()
            loop(0, GROUP, grad_step)
            gb_sends()
            back_sends(sent, plain)
            loop(GROUP, plain, grad_step)
            late_grads()
            loop(0, plain - 1, back_step, 2)
            gb_total()
            back_step([plain - 1])
        else:
            loop(0, plain, held_step, 2)
            loop(0, plain, grad_all)
            ga_sends()
            gb_sends()
            loop(0, plain, back_step, 2)
            gb_total()

        for o in range(1, n):
            gb_send(o).wait_send()
        for o in range(1, ndp):
            ga_copy(o).wait_send()

        @pl.when(has_right)
        def _():
            tag_right.wait_send()
            if role == "lead":
                each(0, gated + 2, lambda h: kv_copy(h).wait_send())
                each(gated + 3, HEADS, lambda h: kv_copy(h).wait_send())
            else:
                each(0, HEADS, lambda h: kv_copy(h).wait_send())
            if shift:
                stat_right.wait_send()

        @pl.when(has_left)
        def _():
            tag_left.wait_send()
            each(0, plain, lambda h: back_copy(h).wait_send())
            if shift:
                each(0, shift, lambda j: pair_copy(j).wait_send())
                each(0, shift, lambda j: local_copy(j).wait_send())
                scal_left.wait_send()

    if chain:
        run("chain", 0)
    else:

        @pl.when(lead)
        def _():
            run("lead", shifts[0])

        @pl.when(jnp.logical_not(lead))
        def _():
            run("follow", shifts[1])


def writer(*refs):
    ins, outs, sem = refs[:4], refs[4:8], refs[8]
    copies = [pltpu.make_async_copy(a, b, sem.at[i]) for i, (a, b) in enumerate(zip(ins, outs))]
    for copy in copies:
        copy.start()
    for copy in copies:
        copy.wait()


def per_device(n, ndp, queries, keys, values, grad_normed, gain, doc_ids):
    batch, length, features = queries.shape
    flat = (length, features)
    hps = HEADS // ndp
    chain = n // 2 > 2
    shifts = (0,) if chain else SHIFTS
    spare = max(shifts + (1,))
    vmem = pltpu.VMEM
    dma = pltpu.SemaphoreType.DMA
    hbm = pl.BlockSpec(memory_space=pltpu.HBM)
    near = pl.BlockSpec(memory_space=pltpu.VMEM)
    big = jax.ShapeDtypeStruct(flat, BF16)
    square = (HEADS, DIM, DIM)
    small = (2, 8, DIM)
    gq, gk, gv, gg = pl.pallas_call(
        functools.partial(kernel, n, ndp, chain, shifts),
        out_shape=(big, big, big, jax.ShapeDtypeStruct((hps, 1, DIM), F32)),
        in_specs=[pl.BlockSpec(memory_space=pltpu.SMEM), hbm, hbm, hbm, hbm, hbm],
        out_specs=(near, near, near, near),
        scratch_shapes=[
            vmem((features,), BF16), vmem((HEADS, 1, DIM), F32),
            vmem(flat, BF16), vmem(flat, BF16), vmem(flat, BF16), vmem(flat, BF16),
            vmem(square, F32), vmem(square, F32),
            vmem(flat, BF16), vmem(flat, F32), vmem(flat, BF16), vmem(square, BF16),
            vmem(square, F32), vmem(square, F32),
            vmem(flat, F32), vmem(flat, F32),
            vmem((8, DIM), F32), vmem((8, DIM), F32), vmem((8, DIM), F32),
            vmem((SPAN, DIM), F32), vmem((SPAN, DIM), F32),
            vmem((HEADS, 1, DIM), F32), vmem((ndp - 1, hps, 1, DIM), F32), vmem((n, hps, 1, DIM), F32),
            vmem((spare, 3, SPAN, DIM), F32), vmem((spare, 3, SPAN, DIM), F32),
            vmem((SPAN, DIM), F32), vmem((SPAN, DIM), F32),
            vmem(small, F32), vmem(small, F32), vmem(small, F32), vmem(small, F32),
            dma((11,)),
            dma((HEADS,)), dma((HEADS,)), dma((HEADS,)), dma((HEADS,)),
            dma((2,)), dma((2,)),
            dma((ndp - 1,)), dma((ndp - 1,)), dma((n - 1,)), dma((n - 1,)),
            dma((spare, 2)), dma((spare, 2)), dma((2,)), dma((2,)),
            pltpu.SemaphoreType.REGULAR,
            pltpu.SemaphoreType.REGULAR,
        ],
        compiler_params=pltpu.CompilerParams(
            collective_id=0, has_side_effects=True, vmem_limit_bytes=40 << 20
        ),
        name="lin_attn_bwd",
    )(
        doc_ids,
        pltpu.with_memory_space_constraint(gain, pltpu.HBM),
        pltpu.with_memory_space_constraint(queries.reshape(flat), pltpu.HBM),
        pltpu.with_memory_space_constraint(keys.reshape(flat), pltpu.HBM),
        pltpu.with_memory_space_constraint(values.reshape(flat), pltpu.HBM),
        pltpu.with_memory_space_constraint(grad_normed.reshape(flat), pltpu.HBM),
    )
    anywhere = pl.BlockSpec(memory_space=pl.ANY)
    gq, gk, gv, gg = pl.pallas_call(
        writer,
        out_shape=(big, big, big, jax.ShapeDtypeStruct((hps, 1, DIM), F32)),
        in_specs=[anywhere] * 4,
        out_specs=(anywhere,) * 4,
        scratch_shapes=[dma((4,))],
        compiler_params=pltpu.CompilerParams(vmem_limit_bytes=1 << 20),
        name="write_out",
    )(gq, gk, gv, gg)
    whole = (batch, length, features)
    return gq.reshape(whole), gk.reshape(whole), gv.reshape(whole), gg.reshape(features // ndp)


def solution(mesh):
    rows = P(("group", "dp"), "ctx", None)
    return jax.shard_map(
        functools.partial(per_device, mesh.shape["ctx"], mesh.shape["dp"]),
        mesh=mesh,
        in_specs=(rows, rows, rows, rows, P(), P(("group", "dp"), "ctx")),
        out_specs=(rows, rows, rows, P(("group", "dp"))),
        check_vma=False,
    )
```

```python
import functools

import jax
import jax.numpy as jnp
from jax import lax
from jax.experimental import pallas as pl
from jax.experimental.pallas import tpu as pltpu
from jax.sharding import PartitionSpec as P

HEADS = 16
DIM = 128
SPAN = 128
SHIFTS = (2, 4)
HELD = 5
GROUP = 4
AHEAD = 2
MESH = pl.DeviceIdType.MESH
F32 = jnp.float32
BF16 = jnp.bfloat16


def dot(a, b, ca, cb):
    return lax.dot_general(a, b, (((ca,), (cb,)), ((), ())), preferred_element_type=F32)


def kernel(
    n, ndp, chain, shifts, doc, gain_hbm, q_hbm, k_hbm, v_hbm, y_hbm,
    gq, gk, gv, gg_out,
    gain_in, gain, q, k, v, y, kvb, kvr, intra, attn, da, stb, qdo, bkr, gkp, gvp,
    tag, tagl, tagr, ssq, inn, gsum, ga, gb, stage, rstage, dsq, dnn, stat, statr, scal, scalr,
    in_sem, ks, kr, bs, br, ts, tr, gas, gar, gbs, gbr, ss, sr, ms, mr, gate, ready,
):
    me = lax.axis_index("ctx")
    mydp = lax.axis_index("dp")
    right, left = lax.rem(me + 1, n), lax.rem(me + n - 1, n)
    has_right, has_left = me < n - 1, me > 0
    lead = lax.rem(mydp, 2) == 0
    twin = mydp + 1 - 2 * lax.rem(mydp, 2)
    hps = HEADS // ndp
    features = HEADS * DIM

    edge, near_end = DIM, (HEADS - AHEAD) * DIM
    parts = [
        [(q_hbm, q, near_end, features), (y_hbm, y, near_end, features)],
        [(k_hbm, k, 0, edge), (v_hbm, v, 0, edge)],
        [(k_hbm, k, near_end, features), (v_hbm, v, near_end, features)],
        [(k_hbm, k, edge, near_end), (v_hbm, v, edge, near_end)],
        [(q_hbm, q, 0, near_end), (y_hbm, y, 0, near_end)],
    ]
    groups = []
    for part in parts:
        group = []
        for src, dst, first, last in part:
            i = 2 * len(groups) + len(group)
            group.append(
                pltpu.make_async_copy(src.at[:, first:last], dst.at[:, first:last], in_sem.at[i])
            )
        groups.append(group)
    groups[2].append(pltpu.make_async_copy(gain_hbm, gain_in, in_sem.at[10]))
    for load in groups[0] + groups[1]:
        load.start()

    def loaded(i):
        for load in groups[i]:
            load.wait()

    barrier = pltpu.get_barrier_semaphore()

    def greet(sem, axis, place, inside):
        @pl.when(inside)
        def _():
            pl.semaphore_signal(sem, inc=1, device_id={axis: place}, device_id_type=MESH)

    for o in range(1, n):
        greet(barrier, "ctx", lax.rem(me + o, n), me + o < n)
    greet(barrier, "ctx", left, has_left)
    for o in range(1, ndp):
        greet(barrier, "dp", lax.rem(mydp + o, ndp), mydp + o < ndp)

    for group in groups[2:]:
        for load in group:
            load.start()

    def cols(h):
        return pl.ds(pl.multiple_of(h * DIM, DIM), DIM)

    def loop(first, last, body, group=GROUP):
        whole = (last - first) // group

        def step(g, _):
            body([first + g * group + i for i in range(group)])
            return 0

        if whole == 1:
            step(0, 0)
        elif whole > 1:
            lax.fori_loop(0, whole, step, 0)
        if first + whole * group < last:
            body(list(range(first + whole * group, last)))

    def each(first, last, body):
        def step(h, _):
            body(h)
            return 0

        if last > first:
            lax.fori_loop(first, last, step, 0)

    def remote(src, dst, s, r, where):
        return pltpu.make_async_remote_copy(
            src_ref=src, dst_ref=dst, send_sem=s, recv_sem=r, device_id=where, device_id_type=MESH
        )

    to_right, to_left = {"ctx": right}, {"ctx": left}

    def kv_copy(h):
        return remote(kvb.at[h], kvr.at[h], ks.at[h], kr.at[h], to_right)

    def back_copy(h):
        return remote(qdo.at[h], bkr.at[h], bs.at[h], br.at[h], to_left)

    def pair_copy(j):
        return remote(stage.at[j, 0:2], rstage.at[j, 0:2], ss.at[j, 0], sr.at[j, 0], to_left)

    def local_copy(j):
        return remote(stage.at[j, 2], rstage.at[j, 2], ss.at[j, 1], sr.at[j, 1], to_left)

    tag_right = remote(tag, tagl, ts.at[0], tr.at[0], to_right)
    tag_left = remote(tag, tagr, ts.at[1], tr.at[1], to_left)
    stat_right = remote(stat, statr, ms.at[0], mr.at[0], to_right)
    scal_left = remote(scal, scalr, ms.at[1], mr.at[1], to_left)

    own = (doc[0, 0] + 1).astype(F32)
    tag[...] = jnp.full((8, 128), own, F32)
    ssq[...] = jnp.zeros_like(ssq)
    inn[...] = jnp.zeros_like(inn)
    dsq[...] = jnp.zeros_like(dsq)
    dnn[...] = jnp.zeros_like(dnn)

    @pl.when(jnp.logical_not(has_left))
    def _():
        tagl[...] = jnp.full((8, 128), -1.0, F32)
        kvr[...] = jnp.zeros_like(kvr)
        statr[...] = jnp.zeros_like(statr)

    @pl.when(jnp.logical_not(has_right))
    def _():
        tagr[...] = jnp.full((8, 128), -1.0, F32)
        bkr[...] = jnp.zeros_like(bkr)

    rows = lax.broadcasted_iota(jnp.int32, (SPAN, SPAN), 0)
    lanes = lax.broadcasted_iota(jnp.int32, (SPAN, SPAN), 1)
    causal = rows >= lanes

    def kv_only(hs):
        for h, m in [(h, dot(k[:, cols(h)], v[:, cols(h)], 0, 0)) for h in hs]:
            kvb[h] = m

    def kv_step(hs):
        kv_only(hs)
        if not chain:

            @pl.when(has_right)
            def _():
                for h in hs:
                    kv_copy(h).start()

    def local_step(hs):
        scores = [dot(q[:, cols(h)], k[:, cols(h)], 1, 1) for h in hs]
        ws = [jnp.where(causal, x, 0.0).astype(BF16) for x in scores]
        outs = [dot(w, v[:, cols(h)], 1, 0) for h, w in zip(hs, ws)]
        for h, w, a in zip(hs, ws, outs):
            intra[:, cols(h)] = w
            attn[:, cols(h)] = a
        return outs

    def sums(terms):
        total = terms[0]
        for term in terms[1:]:
            total = total + term
        return total

    def norm_sums(hs, outs):
        ssq[...] += sums([a * a for a in outs])
        inn[...] += sums([y[:, cols(h)].astype(F32) * gain[h] * a for h, a in zip(hs, outs)])

    def run(role, shift):
        plain = HEADS - shift

        def wire(js, copy):
            @pl.when(has_left)
            def _():
                for j in js:
                    copy(j).start()

        def stage_in(j):
            stage[j, 0] = q[:, cols(plain + j)].astype(F32)
            stage[j, 1] = y[:, cols(plain + j)].astype(F32)

        def need(i):
            if role == "lead":
                loaded(i)

        need(0)
        if role != "lead":
            for i in range(len(groups)):
                loaded(i)
        if shift:
            stage_in(0)
        pl.semaphore_wait(barrier, me + jnp.where(has_right, 1, 0) + mydp)
        if role == "lead":
            wire([0], pair_copy)

        @pl.when(has_right)
        def _():
            tag_right.start()

        @pl.when(has_left)
        def _():
            tag_left.start()

        need(1)
        first_kv = kv_step if role == "lead" else kv_only
        first_kv([0])
        need(2)
        for j in range(shift):
            h = plain + j
            stage[j, 2] = local_step([h])[0]
            if role == "lead":
                wire([j], local_copy)
            if j + 1 < shift:
                stage_in(j + 1)
                if role == "lead":
                    wire([j + 1], pair_copy)

        for o in range(2, n):
            greet(ready, "ctx", lax.rem(me + n - o, n), me >= o)
        for o in range(1, ndp):
            greet(ready, "dp", lax.rem(mydp + ndp - o, ndp), mydp >= o)
        for h in range(HEADS):
            gain[h] = gain_in[h * DIM : (h + 1) * DIM].astype(F32).reshape(1, DIM)
        for h in range(plain, HEADS):
            norm_sums([h], [attn[:, cols(h)]])
        need(3)
        loop(1, plain, first_kv)
        loop(plain, HEADS, kv_only)
        need(4)
        loop(0, plain, local_step)

        later = jnp.where(has_right, n - 2 - me, 0) + ndp - 1 - mydp

        @pl.when(later > 0)
        def _():
            pl.semaphore_wait(ready, later)

        if role == "follow":
            for j in range(shift):
                wire([j], pair_copy)
                wire([j], local_copy)
            pl.semaphore_wait(gate, 1)

            @pl.when(has_right)
            def _():
                each(0, plain, lambda h: kv_copy(h).start())


        @pl.when(has_left)
        def _():
            tag_right.wait_recv()

        @pl.when(has_right)
        def _():
            tag_left.wait_recv()

        from_left = jnp.broadcast_to(tagl[0:1, :] == tag[0:1, :], (DIM, DIM))
        from_right = jnp.broadcast_to(tagr[0:1, :] == tag[0:1, :], (DIM, DIM))

        def state_step(hs):
            @pl.when(has_left)
            def _():
                for h in hs:
                    kv_copy(h).wait_recv()

            states = [jnp.where(from_left, kvr[h], 0.0) for h in hs]
            if chain:
                for h, state in zip(hs, states):
                    kvb[h] = kvb[h] + state

                @pl.when(has_right)
                def _():
                    for h in hs:
                        kv_copy(h).start()

            rounded = [state.astype(BF16) for state in states]
            outs = [attn[:, cols(h)] + dot(q[:, cols(h)], sb, 1, 0) for h, sb in zip(hs, rounded)]
            for h, sb, a in zip(hs, rounded, outs):
                stb[h] = sb
                attn[:, cols(h)] = a
            return outs

        def attn_step(hs):
            norm_sums(hs, state_step(hs))

        def helper_step(js):
            for j in js:
                pair_copy(j).wait_recv()
                local_copy(j).wait_recv()
            kbs = [jnp.where(from_right, kvb[plain + j], 0.0).astype(BF16) for j in js]
            xs = [dot(rstage[j, 0].astype(BF16), kb, 1, 0) for j, kb in zip(js, kbs)]
            olds = [rstage[j, 2] for j in js]
            dsq[...] += sums([(2.0 * a + x) * x for a, x in zip(olds, xs)])
            dnn[...] += sums([rstage[j, 1] * gain[plain + j] * x for j, x in zip(js, xs)])
            for j, a, x in zip(js, olds, xs):
                rstage[j, 2] = a + x

        gated = plain - 5
        if shift:
            for p in range(shift):
                loop(gated * p // shift, gated * (p + 1) // shift, attn_step, 4)

                @pl.when(has_right)
                def _():
                    helper_step([p])

            @pl.when(has_right)
            def _():
                stat[0] = jnp.sum(jnp.transpose(dsq[...]).reshape(16, 8, SPAN), axis=0)
                stat[1] = jnp.sum(jnp.transpose(dnn[...]).reshape(16, 8, SPAN), axis=0)
                stat_right.start()

            attn_step([gated, gated + 1])
            if role == "lead":

                @pl.when(has_right)
                def _():
                    kv_copy(gated + 3).wait_send()

                pl.semaphore_signal(gate, inc=1, device_id={"dp": twin}, device_id_type=MESH)

            attn_step([gated + 2])
            attn_step([gated + 3])
            attn_step([gated + 4])

            @pl.when(has_left)
            def _():
                stat_right.wait_recv()

            extra_sq = jnp.transpose(jnp.broadcast_to(jnp.sum(statr[0], axis=0, keepdims=True), (DIM, SPAN)))
            extra_in = jnp.transpose(jnp.broadcast_to(jnp.sum(statr[1], axis=0, keepdims=True), (DIM, SPAN)))
        else:
            loop(0, HEADS, attn_step)
            extra_sq = extra_in = 0.0

        mean = jnp.broadcast_to(jnp.sum(ssq[...], axis=-1, keepdims=True), (SPAN, DIM)) + extra_sq
        inner = jnp.broadcast_to(jnp.sum(inn[...], axis=-1, keepdims=True), (SPAN, DIM)) + extra_in
        inv = 1.0 / jnp.sqrt(mean / features + 1e-05)
        coef = inner * inv**3 / features

        def da_step(hs):
            ds = []
            for h in hs:
                a = attn[:, cols(h)]
                g = y[:, cols(h)].astype(F32)
                ds.append((g * gain[h] * inv - a * coef).astype(BF16))
            for h, d in zip(hs, ds):
                da[:, cols(h)] = d
            return ds

        def gain_step(hs):
            rows_of = [
                jnp.sum(y[:, cols(h)].astype(F32) * attn[:, cols(h)] * inv, axis=0, keepdims=True) for h in hs
            ]
            for h, row in zip(hs, rows_of):
                gsum[h] = row

        def grad_all(hs):
            grad_step(hs)
            gain_step(hs)

        def held_step(hs):
            for h, m in [(h, dot(q[:, cols(h)], d, 0, 0)) for h, d in zip(hs, da_step(hs))]:
                qdo[h] = m

        def back_sends(first, last):
            @pl.when(has_left)
            def _():
                for h in range(first, last):
                    back_copy(h).start()

        def send_step(hs):
            held_step(hs)
            if role != "chain":

                @pl.when(has_left)
                def _():
                    for h in hs:
                        back_copy(h).start()

        def grad_step(hs):
            ds = [da[:, cols(h)] for h in hs]
            scores = [dot(d, v[:, cols(h)], 1, 1) for h, d in zip(hs, ds)]
            ws = [jnp.where(causal, x, 0.0).astype(BF16) for x in scores]
            far = [dot(d, stb[h], 1, 1) for h, d in zip(hs, ds)]
            vs = [dot(intra[:, cols(h)], d, 0, 0) for h, d in zip(hs, ds)]
            qs = [dot(w, k[:, cols(h)], 1, 0) + f for h, w, f in zip(hs, ws, far)]
            kk = [dot(w, q[:, cols(h)], 0, 0) for h, w in zip(hs, ws)]
            for h, a, b, c in zip(hs, qs, kk, vs):
                gq[:, cols(h)] = a.astype(BF16)
                gkp[:, cols(h)] = b
                gvp[:, cols(h)] = c

        def ga_copy(o):
            to = lax.rem(mydp + o, ndp)
            return remote(
                gsum.at[pl.ds(to * hps, hps)], ga.at[o - 1], gas.at[o - 1], gar.at[o - 1], {"dp": to}
            )

        def gb_send(o):
            return remote(gb.at[me], gb.at[me], gbs.at[o - 1], gbr.at[o - 1], {"ctx": lax.rem(me + o, n)})

        def gb_recv(o):
            source = lax.rem(me + n - o, n)
            return remote(gb.at[source], gb.at[source], gbs.at[o - 1], gbr.at[o - 1], {"ctx": lax.rem(me + o, n)})

        def finish(hs, backs):
            rounded = [back.astype(BF16) for back in backs]
            kk = [gkp[:, cols(h)] + dot(v[:, cols(h)], bb, 1, 1) for h, bb in zip(hs, rounded)]
            vs = [gvp[:, cols(h)] + dot(k[:, cols(h)], bb, 1, 0) for h, bb in zip(hs, rounded)]
            for h, a, b in zip(hs, kk, vs):
                gk[:, cols(h)] = a.astype(BF16)
                gv[:, cols(h)] = b.astype(BF16)

        def back_step(hs):
            @pl.when(has_right)
            def _():
                for h in hs:
                    back_copy(h).wait_recv()

            backs = [jnp.where(from_right, bkr[h], 0.0) for h in hs]
            if chain:
                for h, back in zip(hs, backs):
                    qdo[h] = qdo[h] + back

                @pl.when(has_left)
                def _():
                    for h in hs:
                        back_copy(h).start()

            finish(hs, backs)

        def scal_step():
            scal[0] = jnp.transpose(inv)[0:8]
            scal[1] = jnp.transpose(coef)[0:8]

            @pl.when(has_left)
            def _():
                scal_left.start()

        def late_step(hs):
            state_step(hs)
            da_step(hs)

        def late_sends():
            @pl.when(has_right)
            def _():
                for j in range(shift):
                    kv_copy(plain + j).start()

        def near_step():
                for h in range(plain, HEADS):
                    gsum[h] = jnp.zeros((1, DIM), F32)

                @pl.when(jnp.logical_not(has_left))
                def _():
                    gain_step(list(range(plain, HEADS)))

                @pl.when(has_right)
                def _():
                    scal_left.wait_recv()
                    r_inv = jnp.transpose(jnp.broadcast_to(scalr[0, 0:1], (DIM, SPAN)))
                    r_coef = jnp.transpose(jnp.broadcast_to(scalr[1, 0:1], (DIM, SPAN)))
                    ds = []
                    for j in range(shift):
                        g, a = rstage[j, 1], rstage[j, 2]
                        gsum[plain + j] = gsum[plain + j] + jnp.sum(g * a * r_inv, axis=0, keepdims=True)
                        ds.append((g * gain[plain + j] * r_inv - a * r_coef).astype(BF16))
                    for j, m in [(j, dot(rstage[j, 0].astype(BF16), d, 0, 0)) for j, d in enumerate(ds)]:
                        bkr[plain + j] = m


        def ga_sends():
            for o in range(1, ndp):
                ga_copy(o).start()

        def gb_sends():
            for o in range(1, ndp):
                ga_copy(o).wait_recv()
            mine = gsum[pl.ds(mydp * hps, hps)]
            for o in range(1, ndp):
                mine = mine + ga[o - 1]
            gb[me] = mine
            for o in range(1, n):
                gb_send(o).start()

        def gb_total():
            for o in range(1, n):
                gb_recv(o).wait_recv()
            total = gb[0]
            for i in range(1, n):
                total = total + gb[i]
            gg_out[...] = total

        def near_finish(hs):
            finish(hs, [jnp.where(from_right, bkr[h], 0.0) for h in hs])

        def late_grads():
            loop(plain, HEADS, late_step)
            loop(plain, HEADS, grad_step)
            loop(plain, HEADS, near_finish)

        if role == "lead":
            send_step([0])
            scal_step()
            loop(1, plain, send_step, 2)
            loop(0, plain, grad_all)
            near_step()
            ga_sends()
            loop(0, plain, back_step, 2)
            late_sends()
            gb_sends()
            late_grads()
            gb_total()
        elif role == "follow":
            sent = plain - HELD
            send_step([0])
            scal_step()
            loop(1, sent, send_step, 2)
            loop(sent, plain, held_step, HELD)
            loop(0, plain, gain_step)
            near_step()
            ga_sends()
            late_sends()
            loop(0, GROUP, grad_step)
            gb_sends()
            back_sends(sent, plain)
            loop(GROUP, plain, grad_step)
            late_grads()
            loop(0, plain - 1, back_step, 2)
            gb_total()
            back_step([plain - 1])
        else:
            loop(0, plain, held_step, 2)
            loop(0, plain, grad_all)
            ga_sends()
            gb_sends()
            loop(0, plain, back_step, 2)
            gb_total()

        for o in range(1, n):
            gb_send(o).wait_send()
        for o in range(1, ndp):
            ga_copy(o).wait_send()

        @pl.when(has_right)
        def _():
            tag_right.wait_send()
            if role == "lead":
                each(0, gated + 3, lambda h: kv_copy(h).wait_send())
                each(gated + 4, HEADS, lambda h: kv_copy(h).wait_send())
            else:
                each(0, HEADS, lambda h: kv_copy(h).wait_send())
            if shift:
                stat_right.wait_send()

        @pl.when(has_left)
        def _():
            tag_left.wait_send()
            each(0, plain, lambda h: back_copy(h).wait_send())
            if shift:
                each(0, shift, lambda j: pair_copy(j).wait_send())
                each(0, shift, lambda j: local_copy(j).wait_send())
                scal_left.wait_send()

    if chain:
        run("chain", 0)
    else:

        @pl.when(lead)
        def _():
            run("lead", shifts[0])

        @pl.when(jnp.logical_not(lead))
        def _():
            run("follow", shifts[1])


def writer(*refs):
    ins, outs, sem = refs[:4], refs[4:8], refs[8]
    copies = [pltpu.make_async_copy(a, b, sem.at[i]) for i, (a, b) in enumerate(zip(ins, outs))]
    for copy in copies:
        copy.start()
    for copy in copies:
        copy.wait()


def per_device(n, ndp, queries, keys, values, grad_normed, gain, doc_ids):
    batch, length, features = queries.shape
    flat = (length, features)
    hps = HEADS // ndp
    chain = n // 2 > 2
    shifts = (0,) if chain else SHIFTS
    spare = max(shifts + (1,))
    vmem = pltpu.VMEM
    dma = pltpu.SemaphoreType.DMA
    hbm = pl.BlockSpec(memory_space=pltpu.HBM)
    near = pl.BlockSpec(memory_space=pltpu.VMEM)
    big = jax.ShapeDtypeStruct(flat, BF16)
    square = (HEADS, DIM, DIM)
    small = (2, 8, DIM)
    gq, gk, gv, gg = pl.pallas_call(
        functools.partial(kernel, n, ndp, chain, shifts),
        out_shape=(big, big, big, jax.ShapeDtypeStruct((hps, 1, DIM), F32)),
        in_specs=[pl.BlockSpec(memory_space=pltpu.SMEM), hbm, hbm, hbm, hbm, hbm],
        out_specs=(near, near, near, near),
        scratch_shapes=[
            vmem((features,), BF16), vmem((HEADS, 1, DIM), F32),
            vmem(flat, BF16), vmem(flat, BF16), vmem(flat, BF16), vmem(flat, BF16),
            vmem(square, F32), vmem(square, F32),
            vmem(flat, BF16), vmem(flat, F32), vmem(flat, BF16), vmem(square, BF16),
            vmem(square, F32), vmem(square, F32),
            vmem(flat, F32), vmem(flat, F32),
            vmem((8, DIM), F32), vmem((8, DIM), F32), vmem((8, DIM), F32),
            vmem((SPAN, DIM), F32), vmem((SPAN, DIM), F32),
            vmem((HEADS, 1, DIM), F32), vmem((ndp - 1, hps, 1, DIM), F32), vmem((n, hps, 1, DIM), F32),
            vmem((spare, 3, SPAN, DIM), F32), vmem((spare, 3, SPAN, DIM), F32),
            vmem((SPAN, DIM), F32), vmem((SPAN, DIM), F32),
            vmem(small, F32), vmem(small, F32), vmem(small, F32), vmem(small, F32),
            dma((11,)),
            dma((HEADS,)), dma((HEADS,)), dma((HEADS,)), dma((HEADS,)),
            dma((2,)), dma((2,)),
            dma((ndp - 1,)), dma((ndp - 1,)), dma((n - 1,)), dma((n - 1,)),
            dma((spare, 2)), dma((spare, 2)), dma((2,)), dma((2,)),
            pltpu.SemaphoreType.REGULAR,
            pltpu.SemaphoreType.REGULAR,
        ],
        compiler_params=pltpu.CompilerParams(
            collective_id=0, has_side_effects=True, vmem_limit_bytes=40 << 20
        ),
        name="lin_attn_bwd",
    )(
        doc_ids,
        pltpu.with_memory_space_constraint(gain, pltpu.HBM),
        pltpu.with_memory_space_constraint(queries.reshape(flat), pltpu.HBM),
        pltpu.with_memory_space_constraint(keys.reshape(flat), pltpu.HBM),
        pltpu.with_memory_space_constraint(values.reshape(flat), pltpu.HBM),
        pltpu.with_memory_space_constraint(grad_normed.reshape(flat), pltpu.HBM),
    )
    anywhere = pl.BlockSpec(memory_space=pl.ANY)
    gq, gk, gv, gg = pl.pallas_call(
        writer,
        out_shape=(big, big, big, jax.ShapeDtypeStruct((hps, 1, DIM), F32)),
        in_specs=[anywhere] * 4,
        out_specs=(anywhere,) * 4,
        scratch_shapes=[dma((4,))],
        compiler_params=pltpu.CompilerParams(vmem_limit_bytes=1 << 20),
        name="write_out",
    )(gq, gk, gv, gg)
    whole = (batch, length, features)
    return gq.reshape(whole), gk.reshape(whole), gv.reshape(whole), gg.reshape(features // ndp)


def solution(mesh):
    rows = P(("group", "dp"), "ctx", None)
    return jax.shard_map(
        functools.partial(per_device, mesh.shape["ctx"], mesh.shape["dp"]),
        mesh=mesh,
        in_specs=(rows, rows, rows, rows, P(), P(("group", "dp"), "ctx")),
        out_specs=(rows, rows, rows, P(("group", "dp"))),
        check_vma=False,
    )
```

```python
import functools

import jax
import jax.numpy as jnp
from jax import lax
from jax.experimental import pallas as pl
from jax.experimental.pallas import tpu as pltpu
from jax.sharding import PartitionSpec as P

HEADS = 16
DIM = 128
SPAN = 128
SHIFTS = (2, 4)
HELD = 3
GROUP = 4
MESH = pl.DeviceIdType.MESH
F32 = jnp.float32
BF16 = jnp.bfloat16


def dot(a, b, ca, cb):
    return lax.dot_general(a, b, (((ca,), (cb,)), ((), ())), preferred_element_type=F32)


def kernel(
    n, ndp, chain, shifts, doc, gain_hbm, q_hbm, k_hbm, v_hbm, y_hbm,
    gq, gk, gv, gg_out,
    gain_in, gain, q, k, v, y, kvb, kvr, intra, attn, da, stb, qdo, bkr, gkp, gvp,
    tag, tagl, tagr, ssq, inn, gsum, ga, gb, stage, rstage, dsq, dnn, stat, statr, scal, scalr,
    in_sem, ks, kr, bs, br, ts, tr, gas, gar, gbs, gbr, ss, sr, ms, mr, gate, ready,
):
    me = lax.axis_index("ctx")
    mydp = lax.axis_index("dp")
    right, left = lax.rem(me + 1, n), lax.rem(me + n - 1, n)
    has_right, has_left = me < n - 1, me > 0
    lead = lax.rem(mydp, 2) == 0
    twin = mydp + 1 - 2 * lax.rem(mydp, 2)
    hps = HEADS // ndp
    features = HEADS * DIM

    edge, near_end = GROUP * DIM, (HEADS - GROUP) * DIM
    parts = [
        [(q_hbm, q, near_end, features), (y_hbm, y, near_end, features)],
        [(k_hbm, k, 0, edge), (v_hbm, v, 0, edge)],
        [(k_hbm, k, near_end, features), (v_hbm, v, near_end, features)],
        [(k_hbm, k, edge, near_end), (v_hbm, v, edge, near_end)],
        [(q_hbm, q, 0, near_end), (y_hbm, y, 0, near_end)],
    ]
    groups = []
    for part in parts:
        group = []
        for src, dst, first, last in part:
            i = 2 * len(groups) + len(group)
            group.append(
                pltpu.make_async_copy(src.at[:, first:last], dst.at[:, first:last], in_sem.at[i])
            )
        groups.append(group)
    groups[2].append(pltpu.make_async_copy(gain_hbm, gain_in, in_sem.at[10]))
    for load in groups[0] + groups[1]:
        load.start()

    def loaded(i):
        for load in groups[i]:
            load.wait()

    barrier = pltpu.get_barrier_semaphore()

    def greet(sem, axis, place, inside):
        @pl.when(inside)
        def _():
            pl.semaphore_signal(sem, inc=1, device_id={axis: place}, device_id_type=MESH)

    for o in range(1, n):
        greet(barrier, "ctx", lax.rem(me + o, n), me + o < n)
    greet(barrier, "ctx", left, has_left)
    for o in range(1, ndp):
        greet(barrier, "dp", lax.rem(mydp + o, ndp), mydp + o < ndp)

    for group in groups[2:]:
        for load in group:
            load.start()

    def cols(h):
        return pl.ds(pl.multiple_of(h * DIM, DIM), DIM)

    def loop(first, last, body, group=GROUP):
        whole = (last - first) // group

        def step(g, _):
            body([first + g * group + i for i in range(group)])
            return 0

        if whole == 1:
            step(0, 0)
        elif whole > 1:
            lax.fori_loop(0, whole, step, 0)
        if first + whole * group < last:
            body(list(range(first + whole * group, last)))

    def each(first, last, body):
        def step(h, _):
            body(h)
            return 0

        if last > first:
            lax.fori_loop(first, last, step, 0)

    def remote(src, dst, s, r, where):
        return pltpu.make_async_remote_copy(
            src_ref=src, dst_ref=dst, send_sem=s, recv_sem=r, device_id=where, device_id_type=MESH
        )

    to_right, to_left = {"ctx": right}, {"ctx": left}

    def kv_copy(h):
        return remote(kvb.at[h], kvr.at[h], ks.at[h], kr.at[h], to_right)

    def back_copy(h):
        return remote(qdo.at[h], bkr.at[h], bs.at[h], br.at[h], to_left)

    def pair_copy(j):
        return remote(stage.at[j, 0:2], rstage.at[j, 0:2], ss.at[j, 0], sr.at[j, 0], to_left)

    def local_copy(j):
        return remote(stage.at[j, 2], rstage.at[j, 2], ss.at[j, 1], sr.at[j, 1], to_left)

    tag_right = remote(tag, tagl, ts.at[0], tr.at[0], to_right)
    tag_left = remote(tag, tagr, ts.at[1], tr.at[1], to_left)
    stat_right = remote(stat, statr, ms.at[0], mr.at[0], to_right)
    scal_left = remote(scal, scalr, ms.at[1], mr.at[1], to_left)

    own = (doc[0, 0] + 1).astype(F32)
    tag[...] = jnp.full((8, 128), own, F32)
    ssq[...] = jnp.zeros_like(ssq)
    inn[...] = jnp.zeros_like(inn)
    dsq[...] = jnp.zeros_like(dsq)
    dnn[...] = jnp.zeros_like(dnn)

    @pl.when(jnp.logical_not(has_left))
    def _():
        tagl[...] = jnp.full((8, 128), -1.0, F32)
        kvr[...] = jnp.zeros_like(kvr)
        statr[...] = jnp.zeros_like(statr)

    @pl.when(jnp.logical_not(has_right))
    def _():
        tagr[...] = jnp.full((8, 128), -1.0, F32)
        bkr[...] = jnp.zeros_like(bkr)

    rows = lax.broadcasted_iota(jnp.int32, (SPAN, SPAN), 0)
    lanes = lax.broadcasted_iota(jnp.int32, (SPAN, SPAN), 1)
    causal = rows >= lanes

    def kv_only(hs):
        for h, m in [(h, dot(k[:, cols(h)], v[:, cols(h)], 0, 0)) for h in hs]:
            kvb[h] = m

    def kv_step(hs):
        kv_only(hs)
        if not chain:

            @pl.when(has_right)
            def _():
                for h in hs:
                    kv_copy(h).start()

    def local_step(hs):
        scores = [dot(q[:, cols(h)], k[:, cols(h)], 1, 1) for h in hs]
        ws = [jnp.where(causal, x, 0.0).astype(BF16) for x in scores]
        outs = [dot(w, v[:, cols(h)], 1, 0) for h, w in zip(hs, ws)]
        for h, w, a in zip(hs, ws, outs):
            intra[:, cols(h)] = w
            attn[:, cols(h)] = a
        return outs

    def sums(terms):
        total = terms[0]
        for term in terms[1:]:
            total = total + term
        return total

    def norm_sums(hs, outs):
        ssq[...] += sums([a * a for a in outs])
        inn[...] += sums([y[:, cols(h)].astype(F32) * gain[h] * a for h, a in zip(hs, outs)])

    def run(role, shift):
        plain = HEADS - shift

        def wire(js, copy):
            @pl.when(has_left)
            def _():
                for j in js:
                    copy(j).start()

        loaded(0)
        for j in range(shift):
            stage[j, 0] = q[:, cols(plain + j)].astype(F32)
            stage[j, 1] = y[:, cols(plain + j)].astype(F32)
        loaded(1)
        kv_only([0])
        pl.semaphore_wait(barrier, me + jnp.where(has_right, 1, 0) + mydp)

        @pl.when(has_right)
        def _():
            tag_right.start()

        @pl.when(has_left)
        def _():
            tag_left.start()

        first_kv = kv_step if role == "lead" else kv_only
        if role == "lead":
            wire([0], pair_copy)

            @pl.when(has_right)
            def _():
                kv_copy(0).start()

        loop(1, GROUP, first_kv, GROUP - 1)
        loaded(2)
        for j in range(shift):
            h = plain + j
            stage[j, 2] = local_step([h])[0]
            if role == "lead":
                wire([j], local_copy)
                if j + 1 < shift:
                    wire([j + 1], pair_copy)

        for o in range(2, n):
            greet(ready, "ctx", lax.rem(me + n - o, n), me >= o)
        for o in range(1, ndp):
            greet(ready, "dp", lax.rem(mydp + ndp - o, ndp), mydp >= o)
        for h in range(HEADS):
            gain[h] = gain_in[h * DIM : (h + 1) * DIM].astype(F32).reshape(1, DIM)
        for h in range(plain, HEADS):
            norm_sums([h], [attn[:, cols(h)]])
        loaded(3)
        loop(GROUP, plain, first_kv)
        loop(plain, HEADS, kv_only)
        loaded(4)
        loop(0, plain, local_step)

        later = jnp.where(has_right, n - 2 - me, 0) + ndp - 1 - mydp

        @pl.when(later > 0)
        def _():
            pl.semaphore_wait(ready, later)

        if role == "follow":
            for j in range(shift):
                wire([j], pair_copy)
                wire([j], local_copy)
            pl.semaphore_wait(gate, 1)

            @pl.when(has_right)
            def _():
                each(0, plain, lambda h: kv_copy(h).start())


        @pl.when(has_left)
        def _():
            tag_right.wait_recv()

        @pl.when(has_right)
        def _():
            tag_left.wait_recv()

        from_left = jnp.broadcast_to(tagl[0:1, :] == tag[0:1, :], (DIM, DIM))
        from_right = jnp.broadcast_to(tagr[0:1, :] == tag[0:1, :], (DIM, DIM))

        def state_step(hs):
            @pl.when(has_left)
            def _():
                for h in hs:
                    kv_copy(h).wait_recv()

            states = [jnp.where(from_left, kvr[h], 0.0) for h in hs]
            if chain:
                for h, state in zip(hs, states):
                    kvb[h] = kvb[h] + state

                @pl.when(has_right)
                def _():
                    for h in hs:
                        kv_copy(h).start()

            rounded = [state.astype(BF16) for state in states]
            outs = [attn[:, cols(h)] + dot(q[:, cols(h)], sb, 1, 0) for h, sb in zip(hs, rounded)]
            for h, sb, a in zip(hs, rounded, outs):
                stb[h] = sb
                attn[:, cols(h)] = a
            return outs

        def attn_step(hs):
            norm_sums(hs, state_step(hs))

        def helper_step(js):
            for j in js:
                pair_copy(j).wait_recv()
                local_copy(j).wait_recv()
            kbs = [jnp.where(from_right, kvb[plain + j], 0.0).astype(BF16) for j in js]
            xs = [dot(rstage[j, 0].astype(BF16), kb, 1, 0) for j, kb in zip(js, kbs)]
            olds = [rstage[j, 2] for j in js]
            dsq[...] += sums([(2.0 * a + x) * x for a, x in zip(olds, xs)])
            dnn[...] += sums([rstage[j, 1] * gain[plain + j] * x for j, x in zip(js, xs)])
            for j, a, x in zip(js, olds, xs):
                rstage[j, 2] = a + x

        gated = plain - 5
        if shift:
            for p in range(shift):
                loop(gated * p // shift, gated * (p + 1) // shift, attn_step, 4)

                @pl.when(has_right)
                def _():
                    helper_step([p])

            @pl.when(has_right)
            def _():
                stat[0] = jnp.sum(jnp.transpose(dsq[...]).reshape(16, 8, SPAN), axis=0)
                stat[1] = jnp.sum(jnp.transpose(dnn[...]).reshape(16, 8, SPAN), axis=0)
                stat_right.start()

            attn_step([gated, gated + 1])
            if role == "lead":

                @pl.when(has_right)
                def _():
                    kv_copy(gated + 2).wait_send()

                pl.semaphore_signal(gate, inc=1, device_id={"dp": twin}, device_id_type=MESH)

            attn_step([gated + 2])
            attn_step([gated + 3])
            attn_step([gated + 4])

            @pl.when(has_left)
            def _():
                stat_right.wait_recv()

            extra_sq = jnp.transpose(jnp.broadcast_to(jnp.sum(statr[0], axis=0, keepdims=True), (DIM, SPAN)))
            extra_in = jnp.transpose(jnp.broadcast_to(jnp.sum(statr[1], axis=0, keepdims=True), (DIM, SPAN)))
        else:
            loop(0, HEADS, attn_step)
            extra_sq = extra_in = 0.0

        mean = jnp.broadcast_to(jnp.sum(ssq[...], axis=-1, keepdims=True), (SPAN, DIM)) + extra_sq
        inner = jnp.broadcast_to(jnp.sum(inn[...], axis=-1, keepdims=True), (SPAN, DIM)) + extra_in
        inv = 1.0 / jnp.sqrt(mean / features + 1e-05)
        coef = inner * inv**3 / features

        if shift:
            scal[0] = jnp.transpose(inv)[0:8]
            scal[1] = jnp.transpose(coef)[0:8]

            @pl.when(has_left)
            def _():
                scal_left.start()

        def da_step(hs):
            ds = []
            for h in hs:
                a = attn[:, cols(h)]
                g = y[:, cols(h)].astype(F32)
                ds.append((g * gain[h] * inv - a * coef).astype(BF16))
            for h, d in zip(hs, ds):
                da[:, cols(h)] = d
            return ds

        def gain_step(hs):
            rows_of = [
                jnp.sum(y[:, cols(h)].astype(F32) * attn[:, cols(h)] * inv, axis=0, keepdims=True) for h in hs
            ]
            for h, row in zip(hs, rows_of):
                gsum[h] = row

        def grad_all(hs):
            grad_step(hs)
            gain_step(hs)

        def held_step(hs):
            for h, m in [(h, dot(q[:, cols(h)], d, 0, 0)) for h, d in zip(hs, da_step(hs))]:
                qdo[h] = m

        def back_sends(first, last):
            @pl.when(has_left)
            def _():
                for h in range(first, last):
                    back_copy(h).start()

        def send_step(hs):
            held_step(hs)
            if role != "chain":

                @pl.when(has_left)
                def _():
                    for h in hs:
                        back_copy(h).start()

        def grad_step(hs):
            ds = [da[:, cols(h)] for h in hs]
            scores = [dot(d, v[:, cols(h)], 1, 1) for h, d in zip(hs, ds)]
            ws = [jnp.where(causal, x, 0.0).astype(BF16) for x in scores]
            far = [dot(d, stb[h], 1, 1) for h, d in zip(hs, ds)]
            vs = [dot(intra[:, cols(h)], d, 0, 0) for h, d in zip(hs, ds)]
            qs = [dot(w, k[:, cols(h)], 1, 0) + f for h, w, f in zip(hs, ws, far)]
            kk = [dot(w, q[:, cols(h)], 0, 0) for h, w in zip(hs, ws)]
            for h, a, b, c in zip(hs, qs, kk, vs):
                gq[:, cols(h)] = a.astype(BF16)
                gkp[:, cols(h)] = b
                gvp[:, cols(h)] = c

        def ga_copy(o):
            to = lax.rem(mydp + o, ndp)
            return remote(
                gsum.at[pl.ds(to * hps, hps)], ga.at[o - 1], gas.at[o - 1], gar.at[o - 1], {"dp": to}
            )

        def gb_send(o):
            return remote(gb.at[me], gb.at[me], gbs.at[o - 1], gbr.at[o - 1], {"ctx": lax.rem(me + o, n)})

        def gb_recv(o):
            source = lax.rem(me + n - o, n)
            return remote(gb.at[source], gb.at[source], gbs.at[o - 1], gbr.at[o - 1], {"ctx": lax.rem(me + o, n)})

        def finish(hs, backs):
            rounded = [back.astype(BF16) for back in backs]
            kk = [gkp[:, cols(h)] + dot(v[:, cols(h)], bb, 1, 1) for h, bb in zip(hs, rounded)]
            vs = [gvp[:, cols(h)] + dot(k[:, cols(h)], bb, 1, 0) for h, bb in zip(hs, rounded)]
            for h, a, b in zip(hs, kk, vs):
                gk[:, cols(h)] = a.astype(BF16)
                gv[:, cols(h)] = b.astype(BF16)

        def back_step(hs):
            @pl.when(has_right)
            def _():
                for h in hs:
                    back_copy(h).wait_recv()

            backs = [jnp.where(from_right, bkr[h], 0.0) for h in hs]
            if chain:
                for h, back in zip(hs, backs):
                    qdo[h] = qdo[h] + back

                @pl.when(has_left)
                def _():
                    for h in hs:
                        back_copy(h).start()

            finish(hs, backs)

        def late_step(hs):
            state_step(hs)
            da_step(hs)

        def late_sends():
            @pl.when(has_right)
            def _():
                for j in range(shift):
                    kv_copy(plain + j).start()

        def near_step():
                for h in range(plain, HEADS):
                    gsum[h] = jnp.zeros((1, DIM), F32)

                @pl.when(jnp.logical_not(has_left))
                def _():
                    gain_step(list(range(plain, HEADS)))

                @pl.when(has_right)
                def _():
                    scal_left.wait_recv()
                    r_inv = jnp.transpose(jnp.broadcast_to(scalr[0, 0:1], (DIM, SPAN)))
                    r_coef = jnp.transpose(jnp.broadcast_to(scalr[1, 0:1], (DIM, SPAN)))
                    ds = []
                    for j in range(shift):
                        g, a = rstage[j, 1], rstage[j, 2]
                        gsum[plain + j] = gsum[plain + j] + jnp.sum(g * a * r_inv, axis=0, keepdims=True)
                        ds.append((g * gain[plain + j] * r_inv - a * r_coef).astype(BF16))
                    for j, m in [(j, dot(rstage[j, 0].astype(BF16), d, 0, 0)) for j, d in enumerate(ds)]:
                        bkr[plain + j] = m


        def ga_sends():
            for o in range(1, ndp):
                ga_copy(o).start()

        def gb_sends():
            for o in range(1, ndp):
                ga_copy(o).wait_recv()
            mine = gsum[pl.ds(mydp * hps, hps)]
            for o in range(1, ndp):
                mine = mine + ga[o - 1]
            gb[me] = mine
            for o in range(1, n):
                gb_send(o).start()

        def gb_total():
            for o in range(1, n):
                gb_recv(o).wait_recv()
            total = gb[0]
            for i in range(1, n):
                total = total + gb[i]
            gg_out[...] = total

        def near_finish(hs):
            finish(hs, [jnp.where(from_right, bkr[h], 0.0) for h in hs])

        def late_grads():
            loop(plain, HEADS, late_step)
            loop(plain, HEADS, grad_step)
            loop(plain, HEADS, near_finish)

        if role == "lead":
            send_step([0])
            loop(1, plain, send_step, 2)
            loop(0, plain, grad_all)
            near_step()
            ga_sends()
            loop(0, plain, back_step, 2)
            late_sends()
            gb_sends()
            late_grads()
            gb_total()
        elif role == "follow":
            sent = plain - HELD
            send_step([0])
            loop(1, sent, send_step, 2)
            loop(sent, plain, held_step, HELD)
            loop(0, plain, gain_step)
            near_step()
            ga_sends()
            late_sends()
            loop(0, GROUP, grad_step)
            gb_sends()
            back_sends(sent, plain)
            loop(GROUP, plain, grad_step)
            late_grads()
            loop(0, plain - 1, back_step, 2)
            gb_total()
            back_step([plain - 1])
        else:
            loop(0, plain, held_step, 2)
            loop(0, plain, grad_all)
            ga_sends()
            gb_sends()
            loop(0, plain, back_step, 2)
            gb_total()

        for o in range(1, n):
            gb_send(o).wait_send()
        for o in range(1, ndp):
            ga_copy(o).wait_send()

        @pl.when(has_right)
        def _():
            tag_right.wait_send()
            if role == "lead":
                each(0, gated + 2, lambda h: kv_copy(h).wait_send())
                each(gated + 3, HEADS, lambda h: kv_copy(h).wait_send())
            else:
                each(0, HEADS, lambda h: kv_copy(h).wait_send())
            if shift:
                stat_right.wait_send()

        @pl.when(has_left)
        def _():
            tag_left.wait_send()
            each(0, plain, lambda h: back_copy(h).wait_send())
            if shift:
                each(0, shift, lambda j: pair_copy(j).wait_send())
                each(0, shift, lambda j: local_copy(j).wait_send())
                scal_left.wait_send()

    if chain:
        run("chain", 0)
    else:

        @pl.when(lead)
        def _():
            run("lead", shifts[0])

        @pl.when(jnp.logical_not(lead))
        def _():
            run("follow", shifts[1])


def writer(*refs):
    ins, outs, sem = refs[:4], refs[4:8], refs[8]
    copies = [pltpu.make_async_copy(a, b, sem.at[i]) for i, (a, b) in enumerate(zip(ins, outs))]
    for copy in copies:
        copy.start()
    for copy in copies:
        copy.wait()


def per_device(n, ndp, queries, keys, values, grad_normed, gain, doc_ids):
    batch, length, features = queries.shape
    flat = (length, features)
    hps = HEADS // ndp
    chain = n // 2 > 2
    shifts = (0,) if chain else SHIFTS
    spare = max(shifts + (1,))
    vmem = pltpu.VMEM
    dma = pltpu.SemaphoreType.DMA
    hbm = pl.BlockSpec(memory_space=pltpu.HBM)
    near = pl.BlockSpec(memory_space=pltpu.VMEM)
    big = jax.ShapeDtypeStruct(flat, BF16)
    square = (HEADS, DIM, DIM)
    small = (2, 8, DIM)
    gq, gk, gv, gg = pl.pallas_call(
        functools.partial(kernel, n, ndp, chain, shifts),
        out_shape=(big, big, big, jax.ShapeDtypeStruct((hps, 1, DIM), F32)),
        in_specs=[pl.BlockSpec(memory_space=pltpu.SMEM), hbm, hbm, hbm, hbm, hbm],
        out_specs=(near, near, near, near),
        scratch_shapes=[
            vmem((features,), BF16), vmem((HEADS, 1, DIM), F32),
            vmem(flat, BF16), vmem(flat, BF16), vmem(flat, BF16), vmem(flat, BF16),
            vmem(square, F32), vmem(square, F32),
            vmem(flat, BF16), vmem(flat, F32), vmem(flat, BF16), vmem(square, BF16),
            vmem(square, F32), vmem(square, F32),
            vmem(flat, F32), vmem(flat, F32),
            vmem((8, DIM), F32), vmem((8, DIM), F32), vmem((8, DIM), F32),
            vmem((SPAN, DIM), F32), vmem((SPAN, DIM), F32),
            vmem((HEADS, 1, DIM), F32), vmem((ndp - 1, hps, 1, DIM), F32), vmem((n, hps, 1, DIM), F32),
            vmem((spare, 3, SPAN, DIM), F32), vmem((spare, 3, SPAN, DIM), F32),
            vmem((SPAN, DIM), F32), vmem((SPAN, DIM), F32),
            vmem(small, F32), vmem(small, F32), vmem(small, F32), vmem(small, F32),
            dma((11,)),
            dma((HEADS,)), dma((HEADS,)), dma((HEADS,)), dma((HEADS,)),
            dma((2,)), dma((2,)),
            dma((ndp - 1,)), dma((ndp - 1,)), dma((n - 1,)), dma((n - 1,)),
            dma((spare, 2)), dma((spare, 2)), dma((2,)), dma((2,)),
            pltpu.SemaphoreType.REGULAR,
            pltpu.SemaphoreType.REGULAR,
        ],
        compiler_params=pltpu.CompilerParams(
            collective_id=0, has_side_effects=True, vmem_limit_bytes=40 << 20
        ),
        name="lin_attn_bwd",
    )(
        doc_ids,
        pltpu.with_memory_space_constraint(gain, pltpu.HBM),
        pltpu.with_memory_space_constraint(queries.reshape(flat), pltpu.HBM),
        pltpu.with_memory_space_constraint(keys.reshape(flat), pltpu.HBM),
        pltpu.with_memory_space_constraint(values.reshape(flat), pltpu.HBM),
        pltpu.with_memory_space_constraint(grad_normed.reshape(flat), pltpu.HBM),
    )
    anywhere = pl.BlockSpec(memory_space=pl.ANY)
    gq, gk, gv, gg = pl.pallas_call(
        writer,
        out_shape=(big, big, big, jax.ShapeDtypeStruct((hps, 1, DIM), F32)),
        in_specs=[anywhere] * 4,
        out_specs=(anywhere,) * 4,
        scratch_shapes=[dma((4,))],
        compiler_params=pltpu.CompilerParams(vmem_limit_bytes=1 << 20),
        name="write_out",
    )(gq, gk, gv, gg)
    whole = (batch, length, features)
    return gq.reshape(whole), gk.reshape(whole), gv.reshape(whole), gg.reshape(features // ndp)


def solution(mesh):
    rows = P(("group", "dp"), "ctx", None)
    return jax.shard_map(
        functools.partial(per_device, mesh.shape["ctx"], mesh.shape["dp"]),
        mesh=mesh,
        in_specs=(rows, rows, rows, rows, P(), P(("group", "dp"), "ctx")),
        out_specs=(rows, rows, rows, P(("group", "dp"))),
        check_vma=False,
    )
```

```python
import functools

import jax
import jax.numpy as jnp
from jax import lax
from jax.experimental import pallas as pl
from jax.experimental.pallas import tpu as pltpu
from jax.sharding import PartitionSpec as P

HEADS = 16
DIM = 128
SPAN = 128
SHIFTS = (2, 4)
HELD = 3
GROUP = 4
MESH = pl.DeviceIdType.MESH
F32 = jnp.float32
BF16 = jnp.bfloat16


def dot(a, b, ca, cb):
    return lax.dot_general(a, b, (((ca,), (cb,)), ((), ())), preferred_element_type=F32)


def kernel(
    n, ndp, chain, shifts, doc, gain_hbm, q_hbm, k_hbm, v_hbm, y_hbm,
    gq, gk, gv, gg_out,
    gain_in, gain, q, k, v, y, kvb, kvr, intra, attn, da, stb, qdo, bkr, gkp, gvp,
    tag, tagl, tagr, ssq, inn, gsum, ga, gb, stage, rstage, dsq, dnn, stat, statr, scal, scalr,
    in_sem, ks, kr, bs, br, ts, tr, gas, gar, gbs, gbr, ss, sr, ms, mr, gate, ready,
):
    me = lax.axis_index("ctx")
    mydp = lax.axis_index("dp")
    right, left = lax.rem(me + 1, n), lax.rem(me + n - 1, n)
    has_right, has_left = me < n - 1, me > 0
    lead = lax.rem(mydp, 2) == 0
    twin = mydp + 1 - 2 * lax.rem(mydp, 2)
    hps = HEADS // ndp
    features = HEADS * DIM

    edge, near_end = GROUP * DIM, (HEADS - GROUP) * DIM
    parts = [
        [(q_hbm, q, near_end, features), (y_hbm, y, near_end, features)],
        [(k_hbm, k, 0, edge), (v_hbm, v, 0, edge)],
        [(k_hbm, k, near_end, features), (v_hbm, v, near_end, features)],
        [(k_hbm, k, edge, near_end), (v_hbm, v, edge, near_end)],
        [(q_hbm, q, 0, near_end), (y_hbm, y, 0, near_end)],
    ]
    groups = []
    for part in parts:
        group = []
        for src, dst, first, last in part:
            i = 2 * len(groups) + len(group)
            group.append(
                pltpu.make_async_copy(src.at[:, first:last], dst.at[:, first:last], in_sem.at[i])
            )
        groups.append(group)
    groups[2].append(pltpu.make_async_copy(gain_hbm, gain_in, in_sem.at[10]))
    for load in groups[0] + groups[1]:
        load.start()

    def loaded(i):
        for load in groups[i]:
            load.wait()

    barrier = pltpu.get_barrier_semaphore()

    def greet(sem, axis, place, inside):
        @pl.when(inside)
        def _():
            pl.semaphore_signal(sem, inc=1, device_id={axis: place}, device_id_type=MESH)

    for o in range(1, n):
        greet(barrier, "ctx", lax.rem(me + o, n), me + o < n)
    greet(barrier, "ctx", left, has_left)
    for o in range(1, ndp):
        greet(barrier, "dp", lax.rem(mydp + o, ndp), mydp + o < ndp)

    for group in groups[2:]:
        for load in group:
            load.start()

    def cols(h):
        return pl.ds(pl.multiple_of(h * DIM, DIM), DIM)

    def loop(first, last, body, group=GROUP):
        whole = (last - first) // group

        def step(g, _):
            body([first + g * group + i for i in range(group)])
            return 0

        if whole == 1:
            step(0, 0)
        elif whole > 1:
            lax.fori_loop(0, whole, step, 0)
        if first + whole * group < last:
            body(list(range(first + whole * group, last)))

    def each(first, last, body):
        def step(h, _):
            body(h)
            return 0

        if last > first:
            lax.fori_loop(first, last, step, 0)

    def remote(src, dst, s, r, where):
        return pltpu.make_async_remote_copy(
            src_ref=src, dst_ref=dst, send_sem=s, recv_sem=r, device_id=where, device_id_type=MESH
        )

    to_right, to_left = {"ctx": right}, {"ctx": left}

    def kv_copy(h):
        return remote(kvb.at[h], kvr.at[h], ks.at[h], kr.at[h], to_right)

    def back_copy(h):
        return remote(qdo.at[h], bkr.at[h], bs.at[h], br.at[h], to_left)

    def pair_copy(j):
        return remote(stage.at[j, 0:2], rstage.at[j, 0:2], ss.at[j, 0], sr.at[j, 0], to_left)

    def local_copy(j):
        return remote(stage.at[j, 2], rstage.at[j, 2], ss.at[j, 1], sr.at[j, 1], to_left)

    tag_right = remote(tag, tagl, ts.at[0], tr.at[0], to_right)
    tag_left = remote(tag, tagr, ts.at[1], tr.at[1], to_left)
    stat_right = remote(stat, statr, ms.at[0], mr.at[0], to_right)
    scal_left = remote(scal, scalr, ms.at[1], mr.at[1], to_left)

    own = (doc[0, 0] + 1).astype(F32)
    tag[...] = jnp.full((8, 128), own, F32)
    ssq[...] = jnp.zeros_like(ssq)
    inn[...] = jnp.zeros_like(inn)
    dsq[...] = jnp.zeros_like(dsq)
    dnn[...] = jnp.zeros_like(dnn)

    @pl.when(jnp.logical_not(has_left))
    def _():
        tagl[...] = jnp.full((8, 128), -1.0, F32)
        kvr[...] = jnp.zeros_like(kvr)
        statr[...] = jnp.zeros_like(statr)

    @pl.when(jnp.logical_not(has_right))
    def _():
        tagr[...] = jnp.full((8, 128), -1.0, F32)
        bkr[...] = jnp.zeros_like(bkr)

    rows = lax.broadcasted_iota(jnp.int32, (SPAN, SPAN), 0)
    lanes = lax.broadcasted_iota(jnp.int32, (SPAN, SPAN), 1)
    causal = rows >= lanes

    def kv_only(hs):
        for h, m in [(h, dot(k[:, cols(h)], v[:, cols(h)], 0, 0)) for h in hs]:
            kvb[h] = m

    def kv_step(hs):
        kv_only(hs)
        if not chain:

            @pl.when(has_right)
            def _():
                for h in hs:
                    kv_copy(h).start()

    def local_step(hs):
        scores = [dot(q[:, cols(h)], k[:, cols(h)], 1, 1) for h in hs]
        ws = [jnp.where(causal, x, 0.0).astype(BF16) for x in scores]
        outs = [dot(w, v[:, cols(h)], 1, 0) for h, w in zip(hs, ws)]
        for h, w, a in zip(hs, ws, outs):
            intra[:, cols(h)] = w
            attn[:, cols(h)] = a
        return outs

    def sums(terms):
        total = terms[0]
        for term in terms[1:]:
            total = total + term
        return total

    def norm_sums(hs, outs):
        ssq[...] += sums([a * a for a in outs])
        inn[...] += sums([y[:, cols(h)].astype(F32) * gain[h] * a for h, a in zip(hs, outs)])

    def run(role, shift):
        plain = HEADS - shift

        def wire(js, copy):
            @pl.when(has_left)
            def _():
                for j in js:
                    copy(j).start()

        loaded(0)
        for j in range(shift):
            stage[j, 0] = q[:, cols(plain + j)].astype(F32)
            stage[j, 1] = y[:, cols(plain + j)].astype(F32)
        loaded(1)
        kv_only([0])
        pl.semaphore_wait(barrier, me + jnp.where(has_right, 1, 0) + mydp)

        @pl.when(has_right)
        def _():
            tag_right.start()

        @pl.when(has_left)
        def _():
            tag_left.start()

        first_kv = kv_step if role == "lead" else kv_only
        if role == "lead":
            wire([0], pair_copy)

            @pl.when(has_right)
            def _():
                kv_copy(0).start()

        loop(1, GROUP, first_kv, GROUP - 1)
        loaded(2)
        for j in range(shift):
            h = plain + j
            stage[j, 2] = local_step([h])[0]
            if role == "lead":
                wire([j], local_copy)
                if j + 1 < shift:
                    wire([j + 1], pair_copy)

        for o in range(2, n):
            greet(ready, "ctx", lax.rem(me + n - o, n), me >= o)
        for o in range(1, ndp):
            greet(ready, "dp", lax.rem(mydp + ndp - o, ndp), mydp >= o)
        for h in range(HEADS):
            gain[h] = gain_in[h * DIM : (h + 1) * DIM].astype(F32).reshape(1, DIM)
        for h in range(plain, HEADS):
            norm_sums([h], [attn[:, cols(h)]])
        loaded(3)
        loop(GROUP, plain, first_kv)
        loop(plain, HEADS, kv_only)
        loaded(4)
        loop(0, plain, local_step)

        later = jnp.where(has_right, n - 2 - me, 0) + ndp - 1 - mydp

        @pl.when(later > 0)
        def _():
            pl.semaphore_wait(ready, later)

        if role == "follow":
            for j in range(shift):
                wire([j], pair_copy)
                wire([j], local_copy)
            pl.semaphore_wait(gate, 1)

            @pl.when(has_right)
            def _():
                each(0, plain, lambda h: kv_copy(h).start())


        @pl.when(has_left)
        def _():
            tag_right.wait_recv()

        @pl.when(has_right)
        def _():
            tag_left.wait_recv()

        from_left = jnp.broadcast_to(tagl[0:1, :] == tag[0:1, :], (DIM, DIM))
        from_right = jnp.broadcast_to(tagr[0:1, :] == tag[0:1, :], (DIM, DIM))

        def state_step(hs):
            @pl.when(has_left)
            def _():
                for h in hs:
                    kv_copy(h).wait_recv()

            states = [jnp.where(from_left, kvr[h], 0.0) for h in hs]
            if chain:
                for h, state in zip(hs, states):
                    kvb[h] = kvb[h] + state

                @pl.when(has_right)
                def _():
                    for h in hs:
                        kv_copy(h).start()

            rounded = [state.astype(BF16) for state in states]
            outs = [attn[:, cols(h)] + dot(q[:, cols(h)], sb, 1, 0) for h, sb in zip(hs, rounded)]
            for h, sb, a in zip(hs, rounded, outs):
                stb[h] = sb
                attn[:, cols(h)] = a
            return outs

        def attn_step(hs):
            norm_sums(hs, state_step(hs))

        def helper_step(js):
            for j in js:
                pair_copy(j).wait_recv()
                local_copy(j).wait_recv()
            kbs = [jnp.where(from_right, kvb[plain + j], 0.0).astype(BF16) for j in js]
            xs = [dot(rstage[j, 0].astype(BF16), kb, 1, 0) for j, kb in zip(js, kbs)]
            olds = [rstage[j, 2] for j in js]
            dsq[...] += sums([(2.0 * a + x) * x for a, x in zip(olds, xs)])
            dnn[...] += sums([rstage[j, 1] * gain[plain + j] * x for j, x in zip(js, xs)])
            for j, a, x in zip(js, olds, xs):
                rstage[j, 2] = a + x

        gated = plain - 5
        if shift:
            for p in range(shift):
                loop(gated * p // shift, gated * (p + 1) // shift, attn_step, 4)

                @pl.when(has_right)
                def _():
                    helper_step([p])

            @pl.when(has_right)
            def _():
                stat[0] = jnp.sum(jnp.transpose(dsq[...]).reshape(16, 8, SPAN), axis=0)
                stat[1] = jnp.sum(jnp.transpose(dnn[...]).reshape(16, 8, SPAN), axis=0)
                stat_right.start()

            attn_step([gated, gated + 1])
            if role == "lead":

                @pl.when(has_right)
                def _():
                    kv_copy(gated + 3).wait_send()

                pl.semaphore_signal(gate, inc=1, device_id={"dp": twin}, device_id_type=MESH)

            attn_step([gated + 2])
            attn_step([gated + 3])
            attn_step([gated + 4])

            @pl.when(has_left)
            def _():
                stat_right.wait_recv()

            extra_sq = jnp.transpose(jnp.broadcast_to(jnp.sum(statr[0], axis=0, keepdims=True), (DIM, SPAN)))
            extra_in = jnp.transpose(jnp.broadcast_to(jnp.sum(statr[1], axis=0, keepdims=True), (DIM, SPAN)))
        else:
            loop(0, HEADS, attn_step)
            extra_sq = extra_in = 0.0

        mean = jnp.broadcast_to(jnp.sum(ssq[...], axis=-1, keepdims=True), (SPAN, DIM)) + extra_sq
        inner = jnp.broadcast_to(jnp.sum(inn[...], axis=-1, keepdims=True), (SPAN, DIM)) + extra_in
        inv = 1.0 / jnp.sqrt(mean / features + 1e-05)
        coef = inner * inv**3 / features

        if shift:
            scal[0] = jnp.transpose(inv)[0:8]
            scal[1] = jnp.transpose(coef)[0:8]

            @pl.when(has_left)
            def _():
                scal_left.start()

        def da_step(hs):
            ds = []
            for h in hs:
                a = attn[:, cols(h)]
                g = y[:, cols(h)].astype(F32)
                ds.append((g * gain[h] * inv - a * coef).astype(BF16))
            for h, d in zip(hs, ds):
                da[:, cols(h)] = d
            return ds

        def gain_step(hs):
            rows_of = [
                jnp.sum(y[:, cols(h)].astype(F32) * attn[:, cols(h)] * inv, axis=0, keepdims=True) for h in hs
            ]
            for h, row in zip(hs, rows_of):
                gsum[h] = row

        def grad_all(hs):
            grad_step(hs)
            gain_step(hs)

        def held_step(hs):
            for h, m in [(h, dot(q[:, cols(h)], d, 0, 0)) for h, d in zip(hs, da_step(hs))]:
                qdo[h] = m

        def back_sends(first, last):
            @pl.when(has_left)
            def _():
                for h in range(first, last):
                    back_copy(h).start()

        def send_step(hs):
            held_step(hs)
            if role != "chain":

                @pl.when(has_left)
                def _():
                    for h in hs:
                        back_copy(h).start()

        def grad_step(hs):
            ds = [da[:, cols(h)] for h in hs]
            scores = [dot(d, v[:, cols(h)], 1, 1) for h, d in zip(hs, ds)]
            ws = [jnp.where(causal, x, 0.0).astype(BF16) for x in scores]
            far = [dot(d, stb[h], 1, 1) for h, d in zip(hs, ds)]
            vs = [dot(intra[:, cols(h)], d, 0, 0) for h, d in zip(hs, ds)]
            qs = [dot(w, k[:, cols(h)], 1, 0) + f for h, w, f in zip(hs, ws, far)]
            kk = [dot(w, q[:, cols(h)], 0, 0) for h, w in zip(hs, ws)]
            for h, a, b, c in zip(hs, qs, kk, vs):
                gq[:, cols(h)] = a.astype(BF16)
                gkp[:, cols(h)] = b
                gvp[:, cols(h)] = c

        def ga_copy(o):
            to = lax.rem(mydp + o, ndp)
            return remote(
                gsum.at[pl.ds(to * hps, hps)], ga.at[o - 1], gas.at[o - 1], gar.at[o - 1], {"dp": to}
            )

        def gb_send(o):
            return remote(gb.at[me], gb.at[me], gbs.at[o - 1], gbr.at[o - 1], {"ctx": lax.rem(me + o, n)})

        def gb_recv(o):
            source = lax.rem(me + n - o, n)
            return remote(gb.at[source], gb.at[source], gbs.at[o - 1], gbr.at[o - 1], {"ctx": lax.rem(me + o, n)})

        def finish(hs, backs):
            rounded = [back.astype(BF16) for back in backs]
            kk = [gkp[:, cols(h)] + dot(v[:, cols(h)], bb, 1, 1) for h, bb in zip(hs, rounded)]
            vs = [gvp[:, cols(h)] + dot(k[:, cols(h)], bb, 1, 0) for h, bb in zip(hs, rounded)]
            for h, a, b in zip(hs, kk, vs):
                gk[:, cols(h)] = a.astype(BF16)
                gv[:, cols(h)] = b.astype(BF16)

        def back_step(hs):
            @pl.when(has_right)
            def _():
                for h in hs:
                    back_copy(h).wait_recv()

            backs = [jnp.where(from_right, bkr[h], 0.0) for h in hs]
            if chain:
                for h, back in zip(hs, backs):
                    qdo[h] = qdo[h] + back

                @pl.when(has_left)
                def _():
                    for h in hs:
                        back_copy(h).start()

            finish(hs, backs)

        def late_step(hs):
            state_step(hs)
            da_step(hs)

        def late_sends():
            @pl.when(has_right)
            def _():
                for j in range(shift):
                    kv_copy(plain + j).start()

        def near_step():
                for h in range(plain, HEADS):
                    gsum[h] = jnp.zeros((1, DIM), F32)

                @pl.when(jnp.logical_not(has_left))
                def _():
                    gain_step(list(range(plain, HEADS)))

                @pl.when(has_right)
                def _():
                    scal_left.wait_recv()
                    r_inv = jnp.transpose(jnp.broadcast_to(scalr[0, 0:1], (DIM, SPAN)))
                    r_coef = jnp.transpose(jnp.broadcast_to(scalr[1, 0:1], (DIM, SPAN)))
                    ds = []
                    for j in range(shift):
                        g, a = rstage[j, 1], rstage[j, 2]
                        gsum[plain + j] = gsum[plain + j] + jnp.sum(g * a * r_inv, axis=0, keepdims=True)
                        ds.append((g * gain[plain + j] * r_inv - a * r_coef).astype(BF16))
                    for j, m in [(j, dot(rstage[j, 0].astype(BF16), d, 0, 0)) for j, d in enumerate(ds)]:
                        bkr[plain + j] = m


        def ga_sends():
            for o in range(1, ndp):
                ga_copy(o).start()

        def gb_sends():
            for o in range(1, ndp):
                ga_copy(o).wait_recv()
            mine = gsum[pl.ds(mydp * hps, hps)]
            for o in range(1, ndp):
                mine = mine + ga[o - 1]
            gb[me] = mine
            for o in range(1, n):
                gb_send(o).start()

        def gb_total():
            for o in range(1, n):
                gb_recv(o).wait_recv()
            total = gb[0]
            for i in range(1, n):
                total = total + gb[i]
            gg_out[...] = total

        def near_finish(hs):
            finish(hs, [jnp.where(from_right, bkr[h], 0.0) for h in hs])

        def late_grads():
            loop(plain, HEADS, late_step)
            loop(plain, HEADS, grad_step)
            loop(plain, HEADS, near_finish)

        if role == "lead":
            send_step([0])
            loop(1, plain, send_step, 2)
            loop(0, plain, grad_all)
            near_step()
            ga_sends()
            loop(0, plain, back_step, 2)
            late_sends()
            gb_sends()
            late_grads()
            gb_total()
        elif role == "follow":
            sent = plain - HELD
            send_step([0])
            loop(1, sent, send_step, 2)
            loop(sent, plain, held_step, HELD)
            loop(0, plain, gain_step)
            near_step()
            ga_sends()
            late_sends()
            loop(0, GROUP, grad_step)
            gb_sends()
            back_sends(sent, plain)
            loop(GROUP, plain, grad_step)
            late_grads()
            loop(0, plain - 1, back_step, 2)
            gb_total()
            back_step([plain - 1])
        else:
            loop(0, plain, held_step, 2)
            loop(0, plain, grad_all)
            ga_sends()
            gb_sends()
            loop(0, plain, back_step, 2)
            gb_total()

        for o in range(1, n):
            gb_send(o).wait_send()
        for o in range(1, ndp):
            ga_copy(o).wait_send()

        @pl.when(has_right)
        def _():
            tag_right.wait_send()
            if role == "lead":
                each(0, gated + 3, lambda h: kv_copy(h).wait_send())
                each(gated + 4, HEADS, lambda h: kv_copy(h).wait_send())
            else:
                each(0, HEADS, lambda h: kv_copy(h).wait_send())
            if shift:
                stat_right.wait_send()

        @pl.when(has_left)
        def _():
            tag_left.wait_send()
            each(0, plain, lambda h: back_copy(h).wait_send())
            if shift:
                each(0, shift, lambda j: pair_copy(j).wait_send())
                each(0, shift, lambda j: local_copy(j).wait_send())
                scal_left.wait_send()

    if chain:
        run("chain", 0)
    else:

        @pl.when(lead)
        def _():
            run("lead", shifts[0])

        @pl.when(jnp.logical_not(lead))
        def _():
            run("follow", shifts[1])


def writer(*refs):
    ins, outs, sem = refs[:4], refs[4:8], refs[8]
    copies = [pltpu.make_async_copy(a, b, sem.at[i]) for i, (a, b) in enumerate(zip(ins, outs))]
    for copy in copies:
        copy.start()
    for copy in copies:
        copy.wait()


def per_device(n, ndp, queries, keys, values, grad_normed, gain, doc_ids):
    batch, length, features = queries.shape
    flat = (length, features)
    hps = HEADS // ndp
    chain = n // 2 > 2
    shifts = (0,) if chain else SHIFTS
    spare = max(shifts + (1,))
    vmem = pltpu.VMEM
    dma = pltpu.SemaphoreType.DMA
    hbm = pl.BlockSpec(memory_space=pltpu.HBM)
    near = pl.BlockSpec(memory_space=pltpu.VMEM)
    big = jax.ShapeDtypeStruct(flat, BF16)
    square = (HEADS, DIM, DIM)
    small = (2, 8, DIM)
    gq, gk, gv, gg = pl.pallas_call(
        functools.partial(kernel, n, ndp, chain, shifts),
        out_shape=(big, big, big, jax.ShapeDtypeStruct((hps, 1, DIM), F32)),
        in_specs=[pl.BlockSpec(memory_space=pltpu.SMEM), hbm, hbm, hbm, hbm, hbm],
        out_specs=(near, near, near, near),
        scratch_shapes=[
            vmem((features,), BF16), vmem((HEADS, 1, DIM), F32),
            vmem(flat, BF16), vmem(flat, BF16), vmem(flat, BF16), vmem(flat, BF16),
            vmem(square, F32), vmem(square, F32),
            vmem(flat, BF16), vmem(flat, F32), vmem(flat, BF16), vmem(square, BF16),
            vmem(square, F32), vmem(square, F32),
            vmem(flat, F32), vmem(flat, F32),
            vmem((8, DIM), F32), vmem((8, DIM), F32), vmem((8, DIM), F32),
            vmem((SPAN, DIM), F32), vmem((SPAN, DIM), F32),
            vmem((HEADS, 1, DIM), F32), vmem((ndp - 1, hps, 1, DIM), F32), vmem((n, hps, 1, DIM), F32),
            vmem((spare, 3, SPAN, DIM), F32), vmem((spare, 3, SPAN, DIM), F32),
            vmem((SPAN, DIM), F32), vmem((SPAN, DIM), F32),
            vmem(small, F32), vmem(small, F32), vmem(small, F32), vmem(small, F32),
            dma((11,)),
            dma((HEADS,)), dma((HEADS,)), dma((HEADS,)), dma((HEADS,)),
            dma((2,)), dma((2,)),
            dma((ndp - 1,)), dma((ndp - 1,)), dma((n - 1,)), dma((n - 1,)),
            dma((spare, 2)), dma((spare, 2)), dma((2,)), dma((2,)),
            pltpu.SemaphoreType.REGULAR,
            pltpu.SemaphoreType.REGULAR,
        ],
        compiler_params=pltpu.CompilerParams(
            collective_id=0, has_side_effects=True, vmem_limit_bytes=40 << 20
        ),
        name="lin_attn_bwd",
    )(
        doc_ids,
        pltpu.with_memory_space_constraint(gain, pltpu.HBM),
        pltpu.with_memory_space_constraint(queries.reshape(flat), pltpu.HBM),
        pltpu.with_memory_space_constraint(keys.reshape(flat), pltpu.HBM),
        pltpu.with_memory_space_constraint(values.reshape(flat), pltpu.HBM),
        pltpu.with_memory_space_constraint(grad_normed.reshape(flat), pltpu.HBM),
    )
    anywhere = pl.BlockSpec(memory_space=pl.ANY)
    gq, gk, gv, gg = pl.pallas_call(
        writer,
        out_shape=(big, big, big, jax.ShapeDtypeStruct((hps, 1, DIM), F32)),
        in_specs=[anywhere] * 4,
        out_specs=(anywhere,) * 4,
        scratch_shapes=[dma((4,))],
        compiler_params=pltpu.CompilerParams(vmem_limit_bytes=1 << 20),
        name="write_out",
    )(gq, gk, gv, gg)
    whole = (batch, length, features)
    return gq.reshape(whole), gk.reshape(whole), gv.reshape(whole), gg.reshape(features // ndp)


def solution(mesh):
    rows = P(("group", "dp"), "ctx", None)
    return jax.shard_map(
        functools.partial(per_device, mesh.shape["ctx"], mesh.shape["dp"]),
        mesh=mesh,
        in_specs=(rows, rows, rows, rows, P(), P(("group", "dp"), "ctx")),
        out_specs=(rows, rows, rows, P(("group", "dp"))),
        check_vma=False,
    )
```
